32 devices in a mesh: grp: 2 (over y), gx: 4 (over z), gy: 2 (over x), gz: 2 (over core).
Axes of the slice: x: 2, y: 2, z: 4, core: 2. Of those that a mesh axis runs over, the one named last changes fastest.
Arguments:
- alignment_token_ids: int32 [128, 128], P(('grp', 'gx'), ('gy', 'gz')), parts along dimension 0, may hold values from 0 to 22
- homolog_profile: bfloat16 [128, 128, 256], P(('grp', 'gx'), ('gy', 'gz')), parts along dimension 0, may hold values from -6 to 6
- alignment_mask: int32 [128, 128], P(('grp', 'gx'), ('gy', 'gz')), parts along dimension 0, may hold values 0 or 1
- pair_features: bfloat16 [256, 128, 128], P(('grp', 'gy', 'gz'), 'gx'), parts along dimension 0, may hold values from -4 to 6
- symbol_lookup_weights: bfloat16 [23, 256], replicated, may hold values from -6 to 6
- asking_weights: bfloat16 [256, 256], replicated, may hold values from -0.375 to 0.375
- lookup_weights: bfloat16 [256, 256], replicated, may hold values from -0.375 to 0.375
- content_weights: bfloat16 [256, 256], replicated, may hold values from -0.375 to 0.375
- sigmoid_switch_weights: bfloat16 [256, 256], replicated, may hold values from -0.375 to 0.375
- resulting_weights: bfloat16 [256, 256], replicated, may hold values from -0.75 to 0.75
- pair_bias_matrix: float32 [128, 8], replicated, may hold values from -0.9 to 48
- first_factor_weights: bfloat16 [256, 32], replicated, may hold values from -0.375 to 0.375
- second_factor_weights: bfloat16 [256, 32], replicated, may hold values from -0.375 to 0.375
- outer_mixing_weight: bfloat16 [1024, 128], replicated, may hold values from -1 to 1
- widening_weight: bfloat16 [128, 512], replicated, may hold values from -0.5 to 0.5
- narrowing_weight: bfloat16 [512, 128], replicated, may hold values from -0.375 to 0.375
Outputs:
- profile_refreshed: bfloat16 [128, 128, 256], P(('grp', 'gx'), ('gy', 'gz')), parts along dimension 0
- pair_output: bfloat16 [256, 128, 128], P(('grp', 'gy', 'gz'), 'gx'), parts along dimension 0
The draws below stay inside these ranges and needn't reach their ends.
There are 2 independent parts, one for each index of `grp`. The reference program is written for one: setup_inputs(seed, part) draws one part's arguments, and reference() takes and returns one part's arrays. A program takes and returns all parts, laid end to end along the dimension named above; an argument that names none is the same for every part. Nothing has to cross between parts.
All inputs are finite; a program needn't handle non-finite values. No bound on the sum of `alignment_mask` on one device may be relied on, other than what follows from the above.
Results may differ from the reference program's by a relative error of at most 0.013.
Values may be sent and summed in bfloat16 or wider, within the bound.
No kernel may reach another device: no remote copies, remote signals or barrier semaphores. Data moves between devices by JAX's collectives and lax.ppermute only.
A program may use at most 64 MiB of HBM per device.

```python
import math
import jax
import jax.numpy as jnp
from jax import lax

PROFILE_DEPTH = 256
HEADS = 8
CZ = 128
PRODUCT_WIDTH = 32
CT = 512
SYMBOL_KINDS = 23
HEAD_DIM = 32
HOMOLOG_NUMBER = 64
CHAIN_LENGTH = 128


def draw_pair_features(key, part):
    values_drawn = jnp.clip(jax.random.normal(jax.random.fold_in(key, 11), (CHAIN_LENGTH, CHAIN_LENGTH, CZ), jnp.float32), -4.0, 4.0)
    return values_drawn.astype(jnp.bfloat16)


def draw_pair_bias_matrix(key, part):
    values_drawn = jnp.clip(0.15 * jax.random.normal(jax.random.fold_in(key, 21), (CZ, HEADS), jnp.float32), -0.9, 0.9)
    return values_drawn


def touch_ends(values, rng, smallest, high):
    dims = values.shape
    spot = [jax.random.randint(jax.random.fold_in(rng, axis), (), 0, dims[axis]) for axis in range(len(dims))]
    values = values.at[tuple(spot)].set(smallest)
    longest = dims.index(max(dims))
    spot[longest] = (spot[longest] + 1) % dims[longest]
    return values.at[tuple(spot)].set(high)


def level_of(stream_key, dims, cuts, low, largest):
    def one(position, blocks):
        draws = jax.random.uniform(jax.random.fold_in(jax.random.fold_in(stream_key, 6), position), (blocks,), jnp.float32, low / len(cuts), largest / len(cuts))
        return jnp.repeat(jnp.exp(draws), dims[position] // blocks).reshape((-1,) + (1,) * (len(dims) - position - 1))

    level = one(*cuts[0])
    for cut in cuts[1:]:
        level = level * one(*cut)
    return level


def gaussian(own_key, extent, scale, most, pieces=(), kind=jnp.bfloat16):
    values = scale * jax.random.normal(own_key, extent, jnp.float32)
    if pieces:
        values = values * level_of(own_key, extent, pieces, -0.22, 0.18)
    return jnp.clip(values, -most, most).astype(kind)


def setup_inputs(seed: int = 0, part: int = 0) -> dict:
    arg_keys = jax.random.split(jax.random.key(seed), 17)
    own_keys = jax.random.split(jax.random.fold_in(arg_keys[16], part), 17)
    return {
        "alignment_token_ids": touch_ends(jax.random.randint(own_keys[0], (HOMOLOG_NUMBER, CHAIN_LENGTH), 0, SYMBOL_KINDS), jax.random.fold_in(own_keys[0], 1), 0, SYMBOL_KINDS - 1).astype(jnp.int32),
        "homolog_profile": gaussian(own_keys[1], (HOMOLOG_NUMBER, CHAIN_LENGTH, PROFILE_DEPTH), 1.0, 6.0, ((0, 4), (1, 4))),
        "alignment_mask": touch_ends((jax.random.randint(own_keys[2], (HOMOLOG_NUMBER, CHAIN_LENGTH), 0, 4) < 3).astype(jnp.int32), jax.random.fold_in(own_keys[2], 1), 0, 1),
        "pair_features": draw_pair_features(jax.random.fold_in(jax.random.fold_in(arg_keys[16], part), 71), part),
        "symbol_lookup_weights": gaussian(arg_keys[4], (SYMBOL_KINDS, PROFILE_DEPTH), 1.0, 6.0),
        "asking_weights": gaussian(arg_keys[5], (PROFILE_DEPTH, PROFILE_DEPTH), PROFILE_DEPTH ** -0.5, 0.375),
        "lookup_weights": gaussian(arg_keys[6], (PROFILE_DEPTH, PROFILE_DEPTH), PROFILE_DEPTH ** -0.5, 0.375),
        "content_weights": gaussian(arg_keys[7], (PROFILE_DEPTH, PROFILE_DEPTH), PROFILE_DEPTH ** -0.5, 0.375),
        "sigmoid_switch_weights": gaussian(arg_keys[8], (PROFILE_DEPTH, PROFILE_DEPTH), PROFILE_DEPTH ** -0.5, 0.375),
        "resulting_weights": gaussian(arg_keys[9], (PROFILE_DEPTH, PROFILE_DEPTH), (PROFILE_DEPTH // 4) ** -0.5, 0.75),
        "pair_bias_matrix": draw_pair_bias_matrix(jax.random.fold_in(arg_keys[16], 71), part),
        "first_factor_weights": gaussian(arg_keys[11], (PROFILE_DEPTH, PRODUCT_WIDTH), PROFILE_DEPTH ** -0.5, 0.375),
        "second_factor_weights": gaussian(arg_keys[12], (PROFILE_DEPTH, PRODUCT_WIDTH), PROFILE_DEPTH ** -0.5, 0.375),
        "outer_mixing_weight": gaussian(arg_keys[13], (PRODUCT_WIDTH * PRODUCT_WIDTH, CZ), PRODUCT_WIDTH ** -0.5, 1.0),
        "widening_weight": gaussian(arg_keys[14], (CZ, CT), CZ ** -0.5, 0.5),
        "narrowing_weight": gaussian(arg_keys[15], (CT, CZ), (CT // 2) ** -0.5, 0.375),
    }


HIGHEST_PRECISION = lax.Precision.HIGHEST

def standardize_lastaxis(values):
    average = lax.optimization_barrier(jnp.mean(values, axis=-1, keepdims=True))
    centred = values - average
    return centred * lax.rsqrt(lax.optimization_barrier(jnp.mean(centred * centred, axis=-1, keepdims=True)) + 1e-05)

def reference(alignment_token_ids, homolog_profile, alignment_mask, pair_features, symbol_lookup_weights, asking_weights, lookup_weights, content_weights, sigmoid_switch_weights, resulting_weights, pair_bias_matrix, first_factor_weights, second_factor_weights, outer_mixing_weight, widening_weight, narrowing_weight):
    profile_arriving = homolog_profile.astype(jnp.float32) + symbol_lookup_weights.astype(jnp.float32)[alignment_token_ids]
    standardized_profile = standardize_lastaxis(profile_arriving).astype(jnp.bfloat16).reshape(HOMOLOG_NUMBER * CHAIN_LENGTH, PROFILE_DEPTH)

    def project(weight):
        return jnp.dot(standardized_profile, weight, preferred_element_type=jnp.float32).astype(jnp.bfloat16).reshape(HOMOLOG_NUMBER, CHAIN_LENGTH, HEADS, HEAD_DIM)
    queries = project(asking_weights)
    keys_all = project(lookup_weights)
    values_all = project(content_weights)
    sigmoid_switch = jax.nn.sigmoid(jnp.dot(standardized_profile, sigmoid_switch_weights, preferred_element_type=jnp.float32)).reshape(HOMOLOG_NUMBER, CHAIN_LENGTH, PROFILE_DEPTH)
    pair_bias = jnp.einsum('ijc,ch->ihj', standardize_lastaxis(pair_features.astype(jnp.float32)), pair_bias_matrix, precision=HIGHEST_PRECISION)
    mask_penalty = (alignment_mask.astype(jnp.float32) - 1.0) * 1000000000.0

    def row_attention(row_parts):
        query_row, key_row, value_row, penalty_row = row_parts
        scores = jnp.einsum('ihd,jhd->ihj', query_row.astype(jnp.float32), key_row.astype(jnp.float32), precision=HIGHEST_PRECISION) * HEAD_DIM ** (-0.5)
        scores = scores + pair_bias + penalty_row[None, None, :]
        top = lax.optimization_barrier(jnp.max(scores, axis=-1, keepdims=True))
        exp_scores = jnp.exp(scores - top)
        aggregate = lax.optimization_barrier(jnp.sum(exp_scores, axis=-1))
        weights = exp_scores.astype(jnp.bfloat16)
        accumulated = jnp.einsum('ihj,jhd->ihd', weights.astype(jnp.float32), value_row.astype(jnp.float32), precision=HIGHEST_PRECISION)
        return (accumulated / aggregate[:, :, None]).reshape(CHAIN_LENGTH, PROFILE_DEPTH)
    softmax_combined = lax.map(row_attention, (queries, keys_all, values_all, mask_penalty))
    switched_result = (sigmoid_switch * softmax_combined).astype(jnp.bfloat16).reshape(HOMOLOG_NUMBER * CHAIN_LENGTH, PROFILE_DEPTH)
    profile_refreshed = (profile_arriving + jnp.dot(switched_result, resulting_weights, preferred_element_type=jnp.float32).reshape(HOMOLOG_NUMBER, CHAIN_LENGTH, PROFILE_DEPTH)).astype(jnp.bfloat16)
    averaged_products = standardize_lastaxis(profile_refreshed.astype(jnp.float32)).astype(jnp.bfloat16).reshape(HOMOLOG_NUMBER * CHAIN_LENGTH, PROFILE_DEPTH)
    mask_floating = alignment_mask.astype(jnp.float32)
    left_side = (jnp.dot(averaged_products, first_factor_weights, preferred_element_type=jnp.float32).reshape(HOMOLOG_NUMBER, CHAIN_LENGTH, PRODUCT_WIDTH) * mask_floating[:, :, None]).astype(jnp.bfloat16).reshape(HOMOLOG_NUMBER, CHAIN_LENGTH * PRODUCT_WIDTH)
    right_side = (jnp.dot(averaged_products, second_factor_weights, preferred_element_type=jnp.float32).reshape(HOMOLOG_NUMBER, CHAIN_LENGTH, PRODUCT_WIDTH) * mask_floating[:, :, None]).astype(jnp.bfloat16).reshape(HOMOLOG_NUMBER, CHAIN_LENGTH * PRODUCT_WIDTH)
    pair_count = jnp.dot(mask_floating.T, mask_floating, precision=HIGHEST_PRECISION)
    panel_rows = math.gcd(CHAIN_LENGTH, 16)

    def outer_panel(panel_index):
        left_rows = lax.dynamic_slice_in_dim(left_side, panel_index * (panel_rows * PRODUCT_WIDTH), panel_rows * PRODUCT_WIDTH, 1)
        outer_block = jnp.dot(left_rows.T, right_side, preferred_element_type=jnp.float32).astype(jnp.bfloat16)
        outer_block = outer_block.reshape(panel_rows, PRODUCT_WIDTH, CHAIN_LENGTH, PRODUCT_WIDTH).transpose(0, 2, 1, 3).reshape(panel_rows * CHAIN_LENGTH, PRODUCT_WIDTH * PRODUCT_WIDTH)
        return jnp.dot(outer_block, outer_mixing_weight, preferred_element_type=jnp.float32).reshape(panel_rows, CHAIN_LENGTH, CZ)
    mixed_pair = lax.map(outer_panel, jnp.arange(CHAIN_LENGTH // panel_rows, dtype=jnp.int32)).reshape(CHAIN_LENGTH, CHAIN_LENGTH, CZ)
    pair_mid = pair_features.astype(jnp.float32) + mixed_pair / (pair_count[:, :, None] + 1.0)
    trans_rows = standardize_lastaxis(pair_mid).astype(jnp.bfloat16).reshape(CHAIN_LENGTH * CHAIN_LENGTH, CZ)
    expanded = jax.nn.relu(jnp.dot(trans_rows, widening_weight, preferred_element_type=jnp.float32)).astype(jnp.bfloat16)
    pair_output = (pair_mid + jnp.dot(expanded, narrowing_weight, preferred_element_type=jnp.float32).reshape(CHAIN_LENGTH, CHAIN_LENGTH, CZ)).astype(jnp.bfloat16)
    return (profile_refreshed, pair_output)
```

```python
import functools

import jax
import jax.numpy as jnp
from jax import lax
from jax.experimental import pallas as pl
from jax.experimental.pallas import tpu as pltpu
from jax.sharding import PartitionSpec as P


LANES = 128
F32 = jnp.float32
BF16 = jnp.bfloat16


def iota(shape, dim):
    return lax.broadcasted_iota(jnp.int32, shape, dim)


def standardize(values):
    average = jnp.mean(values, axis=-1, keepdims=True)
    centred = values - average
    return centred * lax.rsqrt(jnp.mean(centred * centred, axis=-1, keepdims=True) + 1e-05)


def dot(left, right, contract=(1, 0), precision=None):
    return lax.dot_general(
        left,
        right,
        (((contract[0],), (contract[1],)), ((), ())),
        preferred_element_type=F32,
        precision=precision,
    )


def tiling_matrix(rows, columns):
    return (iota((rows, columns), 1) % rows == iota((rows, columns), 0)).astype(BF16)


def call(body, outs, scratch=(), flops=0, data=0, name=None, operands=0, smem=0):
    return pl.pallas_call(
        body,
        out_shape=outs,
        scratch_shapes=scratch,
        cost_estimate=pl.CostEstimate(flops=flops, bytes_accessed=data, transcendentals=0),
        name=name,
    )


def embed_kernel(ids_ref, mask_ref, profile_ref, table_ref, msg_ref, arriving_ref, padded):
    sequences, residues, features = profile_ref.shape
    kinds = table_ref.shape[0]
    padded[...] = jnp.zeros_like(padded)
    padded[0:kinds, :] = table_ref[...]
    columns = ids_ref[...].astype(F32).T
    labels = iota((residues, padded.shape[0]), 1).astype(F32)
    hot = [
        (columns[:, s : s + 1] == labels).astype(F32).astype(BF16) for s in range(sequences)
    ]
    rows = sequences * residues
    arriving = profile_ref[...].reshape(rows, features).astype(F32) + dot(
        jnp.concatenate(hot, axis=0), padded[...]
    )
    arriving_ref[...] = arriving
    msg_ref[0:rows, :] = standardize(arriving).astype(BF16)
    mask = mask_ref[...].astype(F32).astype(BF16)
    msg_ref[rows:, :] = dot(mask, tiling_matrix(residues, features)).astype(BF16)


def bias_kernel(pair_ref, matrix_ref, out_ref):
    rows, columns, width = pair_ref.shape
    normed = standardize(pair_ref[...].reshape(rows * columns, width).astype(F32))
    bias = dot(matrix_ref[...], normed, (1, 1), lax.Precision.HIGHEST)
    for target in range(out_ref.shape[0]):
        out_ref[target] = bias


def project_kernel(position, *refs):
    blocks = len(position)
    msgs = refs[:blocks]
    wq_ref, wk_ref, wv_ref, wg_ref, q_ref, k_ref, v_ref, g_ref, pen_ref = refs[blocks:]
    sequences, residues, features = q_ref.shape
    rows = sequences * residues
    total = pen_ref.shape[1]
    x_own, c_own = lax.axis_index("gy"), lax.axis_index("gz")
    own = msgs[0][0:rows, :]
    q_ref[...] = dot(own, wq_ref[...]).astype(BF16).reshape(q_ref.shape)
    g_ref[...] = jax.nn.sigmoid(dot(own, wg_ref[...])).reshape(g_ref.shape)
    lane_block = iota((sequences, total), 1) // residues
    present = jnp.zeros((sequences, total), F32)
    for msg, (shift_y, shift_z, size_y, size_z) in zip(msgs, position):
        block = lax.rem(x_own - shift_y + size_y, size_y) * size_z + lax.rem(
            c_own - shift_z + size_z, size_z
        )
        where = pl.ds(pl.multiple_of(block * residues, residues), residues)
        normed = msg[0:rows, :]
        k_ref[:, where, :] = dot(normed, wk_ref[...]).astype(BF16).reshape(q_ref.shape)
        v_ref[:, where, :] = dot(normed, wv_ref[...]).astype(BF16).reshape(q_ref.shape)
        tiled = msg[rows : rows + sequences, :].astype(F32)
        while tiled.shape[1] < total:
            tiled = jnp.concatenate([tiled, tiled], axis=1)
        present = jnp.where(lane_block == block, tiled[:, 0:total], present)
    pen_ref[...] = (present - 1.0) * 1000000000.0


def attend_kernel(
    heads,
    q_ref,
    k_ref,
    v_ref,
    g_ref,
    pen_ref,
    bias_ref,
    arriving_ref,
    mask_ref,
    wr_ref,
    wf_ref,
    ws_ref,
    profile_ref,
    left_ref,
    right_ref,
    spread,
    bias,
    gated,
    leftish,
    rightish,
):
    sequences, residues, features = q_ref.shape
    total = k_ref.shape[1]
    size = features // heads
    per = LANES // size
    fit = LANES // residues
    groups = bias_ref.shape[0]
    lane = iota((heads, LANES), 1) // residues
    for i in range(residues):
        tile, inner = divmod(i, fit)
        for column in range(total // LANES):
            value = None
            for slot in range(fit):
                source = bias_ref[
                    column * fit + slot, :, tile * LANES : (tile + 1) * LANES
                ]
                shift = ((slot - inner) % fit) * residues
                if shift:
                    source = pltpu.roll(source, shift, 1)
                value = source if value is None else jnp.where(lane == slot, source, value)
            spread[i, :, column * LANES : (column + 1) * LANES] = value
    for h in range(heads):
        bias[h * residues : (h + 1) * residues, :] = spread[:, h, :]
    scale = size ** (-0.5)
    span = per * residues
    own_lanes = iota((span, LANES), 0) // residues == iota((span, LANES), 1) // size
    small_lanes = [iota((residues, LANES), 1) // size == p for p in range(per)]

    def one(s, carry):
        penalty = pen_ref[pl.ds(s, 1), :]
        for part in range(heads // per):
            lanes = slice(part * LANES, (part + 1) * LANES)
            query = q_ref[s, :, lanes]
            stacked = jnp.concatenate([query] * per, axis=0)
            stacked = jnp.where(own_lanes, stacked, jnp.zeros_like(stacked))
            scores = dot(stacked, k_ref[s, :, lanes], (1, 1)) * scale
            scores = scores + bias[part * span : (part + 1) * span, :] + penalty
            top = jnp.max(scores, axis=1, keepdims=True)
            weights = jnp.exp(scores - top)
            aggregate = jnp.sum(weights, axis=1, keepdims=True)
            mixed = dot(weights.astype(BF16), v_ref[s, :, lanes])
            value = mixed[0:residues, :]
            below = jnp.broadcast_to(aggregate[0:residues, :], (residues, LANES))
            for p in range(1, per):
                rows = slice(p * residues, (p + 1) * residues)
                value = jnp.where(small_lanes[p], mixed[rows, :], value)
                below = jnp.where(small_lanes[p], aggregate[rows, :], below)
            gated[s, :, lanes] = (g_ref[s, :, lanes] * (value / below)).astype(BF16)
        return carry

    lax.fori_loop(0, sequences, one, 0, unroll=2)

    rows = sequences * residues
    refreshed = (
        arriving_ref[...] + dot(gated[...].reshape(rows, features), wr_ref[...])
    ).astype(BF16)
    profile_ref[...] = refreshed.reshape(profile_ref.shape)
    normed = standardize(refreshed.astype(F32)).astype(BF16)
    leftish[...] = dot(normed, wf_ref[...]).reshape(leftish.shape)
    width = ws_ref.shape[0]
    for s in range(sequences):
        piece = normed[s * residues : (s + 1) * residues, :]
        rightish[s] = dot(ws_ref[...], jnp.concatenate([piece] * fit, axis=0), (1, 1))
    mask = mask_ref[...].astype(F32).astype(BF16)
    wide = residues * width
    expand = (iota((residues, wide), 1) // width == iota((residues, wide), 0)).astype(BF16)
    left_mask = dot(mask, expand)
    right_mask = dot(mask, tiling_matrix(residues, width * residues))
    for tile in range(wide // LANES):
        lanes = slice(tile * LANES, (tile + 1) * LANES)
        for source, count, step, target, present in (
            (leftish, LANES // width, width, left_ref, left_mask),
            (rightish, fit, residues, right_ref, right_mask),
        ):
            group = iota((sequences, LANES), 1) // step
            value = source[:, tile * count, :]
            for p in range(1, count):
                value = jnp.where(group == p, source[:, tile * count + p, :], value)
            target[:, lanes] = (value * present[:, lanes]).astype(BF16)
    left_ref[:, wide:] = right_mask[:, 0:LANES].astype(BF16)
    right_ref[:, wide:] = right_mask[:, 0:LANES].astype(BF16)


def block_kernel(mix_ref, out_ref, wide):
    width, other, pair_width = mix_ref.shape
    fit = LANES // width
    wide[...] = mix_ref[...].astype(F32)
    for d in range(other):
        piece = wide[:, d, :].astype(BF16)
        blank = jnp.zeros_like(piece)
        for p in range(fit):
            rows = slice((d * fit + p) * width, (d * fit + p + 1) * width)
            out_ref[rows, :] = jnp.concatenate(
                [piece if q == p else blank for q in range(fit)], axis=1
            )


def pair_kernel(left_from, right_from, *refs):
    lefts = refs[: len(left_from)]
    rights = refs[len(left_from) : len(left_from) + len(right_from)]
    (pair_ref, block_ref, w1_ref, w2_ref, out_ref, left, right, stacked, middle) = refs[
        len(left_from) + len(right_from) :
    ]
    sequences = lefts[0].shape[0]
    rows, columns, pair_width = pair_ref.shape
    z_own, x_own, c_own = (lax.axis_index(n) for n in ("gx", "gy", "gz"))
    for ref, other in zip(lefts, left_from):
        start = (z_own ^ other) * sequences
        left[pl.ds(pl.multiple_of(start, sequences), sequences), :] = ref[...]
    for ref, (shift_y, shift_z, size_y, size_z) in zip(rights, right_from):
        block = lax.rem(x_own - shift_y + size_y, size_y) * size_z + lax.rem(
            c_own - shift_z + size_z, size_z
        )
        right[pl.ds(pl.multiple_of(block * sequences, sequences), sequences), :] = ref[...]
    wide = left.shape[1] - LANES
    width = wide // rows
    fit = LANES // width
    depth = wide // columns
    count = dot(right[:, wide:], left[:, wide:], (0, 0))[0:columns, :]
    share = 1.0 / (count + 1.0)
    flipped = right[:, 0:wide].T
    tiles = wide // LANES
    pack = 2 if tiles % 2 == 0 else 1
    for start in range(0, tiles, pack):
        outer = dot(flipped, left[:, start * LANES : (start + pack) * LANES]).astype(BF16)
        for q in range(pack):
            for d in range(depth):
                stacked[
                    (start + q) * columns : (start + q + 1) * columns,
                    d * LANES : (d + 1) * LANES,
                ] = outer[d * columns : (d + 1) * columns, q * LANES : (q + 1) * LANES]
    mixed = dot(stacked[...], block_ref[...])
    for i in range(rows):
        tile, inner = divmod(i, fit)
        part = mixed[
            tile * columns : (tile + 1) * columns,
            inner * pair_width : (inner + 1) * pair_width,
        ]
        middle[i] = pair_ref[i].astype(F32) + part * share[:, i : i + 1]
    flat = middle[...].reshape(rows * columns, pair_width)
    normed = standardize(flat).astype(BF16)
    hidden = jnp.maximum(dot(normed, w1_ref[...]), 0.0).astype(BF16)
    out_ref[...] = (flat + dot(hidden, w2_ref[...])).astype(BF16).reshape(out_ref.shape)


def local(
    sizes,
    alignment_token_ids,
    homolog_profile,
    alignment_mask,
    pair_features,
    symbol_lookup_weights,
    asking_weights,
    lookup_weights,
    content_weights,
    sigmoid_switch_weights,
    resulting_weights,
    pair_bias_matrix,
    first_factor_weights,
    second_factor_weights,
    outer_mixing_weight,
    widening_weight,
    narrowing_weight,
):
    size_x, size_y, size_z = sizes
    sequences, residues, features = homolog_profile.shape
    heads = pair_bias_matrix.shape[1]
    width = first_factor_weights.shape[1]
    pair_rows, pair_columns, pair_width = pair_features.shape
    total = residues * size_y * size_z
    rows = sequences * residues
    shape = jax.ShapeDtypeStruct

    msg, arriving = call(
        embed_kernel,
        (shape((rows + sequences, features), BF16), shape((rows, features), F32)),
        [pltpu.VMEM((LANES, features), BF16)],
        flops=2 * rows * LANES * features,
        data=rows * features * 8,
        name="embed",
    )(alignment_token_ids, alignment_mask, homolog_profile, symbol_lookup_weights)

    def shift(value, axis, count, step):
        return lax.ppermute(value, axis, [(n, (n + step) % count) for n in range(count)])

    far = [msg] + [shift(msg, "gy", size_y, r) for r in range(1, size_y)]
    position, msgs = [], []
    for r in range(size_y):
        for t in range(size_z):
            position.append((r, t, size_y, size_z))
            msgs.append(far[r] if t == 0 else shift(far[r], "gz", size_z, t))

    bias_local = call(
        bias_kernel,
        shape((size_x, heads, pair_rows * pair_columns), F32),
        flops=2 * 6 * pair_rows * pair_columns * pair_width * LANES,
        data=pair_rows * pair_columns * pair_width * 2,
        name="bias",
    )(pair_features, pair_bias_matrix.T)
    bias_all = lax.all_to_all(bias_local, "gx", 0, 0, tiled=True)

    three = (sequences, residues, features)
    keys = (sequences, total, features)
    queries, keys, values, gates, penalty = call(
        functools.partial(project_kernel, tuple(position)),
        (
            shape(three, BF16),
            shape(keys, BF16),
            shape(keys, BF16),
            shape(three, F32),
            shape((sequences, total), F32),
        ),
        flops=2 * sequences * (total + residues) * features * features * 2,
        data=sequences * total * features * 6,
        name="project",
    )(*msgs, asking_weights, lookup_weights, content_weights, sigmoid_switch_weights)

    wide = residues * width
    message = shape((sequences, wide + LANES), BF16)
    refreshed, left_own, right_own = call(
        functools.partial(attend_kernel, heads),
        (shape(three, BF16), message, message),
        [
            pltpu.VMEM((residues, heads, total), F32),
            pltpu.VMEM((heads * residues, total), F32),
            pltpu.VMEM(three, BF16),
            pltpu.VMEM((sequences, residues, LANES), F32),
            pltpu.VMEM((sequences, width, LANES), F32),
        ],
        flops=4 * sequences * heads * residues * total * LANES,
        data=sequences * total * features * 4,
        name="attend",
    )(
        queries,
        keys,
        values,
        gates,
        penalty,
        bias_all,
        arriving,
        alignment_mask,
        resulting_weights,
        jnp.tile(first_factor_weights, (1, LANES // width)),
        second_factor_weights.T,
    )

    lefts = [left_own] + [
        lax.ppermute(left_own, "gx", [(n, n ^ m) for n in range(size_x)])
        for m in range(1, size_x)
    ]
    right_from, rights = [], []
    blocks = size_y * size_z
    for r in range(size_y):
        pairs = []
        for a in range(size_x):
            for b in range(blocks):
                to = ((a // size_z + r) % size_y) * size_z + a % size_z
                pairs.append((a * blocks + b, b * blocks + to))
        got = lax.ppermute(right_own, ("gx", "gy", "gz"), pairs)
        for t in range(size_z):
            right_from.append((r, t, size_y, size_z))
            rights.append(got if t == 0 else shift(got, "gz", size_z, t))

    fit = LANES // width
    block = call(
        block_kernel,
        shape((width * width * fit, pair_width * fit), BF16),
        [pltpu.VMEM((width, width, pair_width), F32)],
        data=width * width * fit * pair_width * fit * 2,
        name="block",
    )(outer_mixing_weight.reshape(width, width, pair_width))

    depth = sequences * size_x
    pair_output = call(
        functools.partial(pair_kernel, tuple(range(size_x)), tuple(right_from)),
        shape(pair_features.shape, BF16),
        [
            pltpu.VMEM((depth, wide + LANES), BF16),
            pltpu.VMEM((depth, wide + LANES), BF16),
            pltpu.VMEM((pair_rows // fit * pair_columns, width * LANES), BF16),
            pltpu.VMEM(pair_features.shape, F32),
        ],
        flops=2 * pair_rows * pair_columns * width * width * pair_width * fit,
        data=width * width * fit * pair_width * fit * 2,
        name="pair",
    )(*lefts, *rights, pair_features, block, widening_weight, narrowing_weight)
    return refreshed, pair_output


def solution(mesh):
    sizes = tuple(mesh.shape[name] for name in ("gx", "gy", "gz"))
    assert sizes[0] == sizes[1] * sizes[2] and sizes[0] & (sizes[0] - 1) == 0
    in_specs = (
        P(("grp", "gx"), ("gy", "gz")),
        P(("grp", "gx"), ("gy", "gz"), None),
        P(("grp", "gx"), ("gy", "gz")),
        P(("grp", "gy", "gz"), "gx", None),
    ) + (P(),) * 12
    out_specs = (P(("grp", "gx"), ("gy", "gz"), None), P(("grp", "gy", "gz"), "gx", None))
    return jax.shard_map(
        functools.partial(local, sizes),
        mesh=mesh,
        in_specs=in_specs,
        out_specs=out_specs,
        check_vma=False,
    )
```

```python
import functools
import math

import jax
import jax.numpy as jnp
from jax import lax
from jax.experimental import pallas as pl
from jax.experimental.pallas import tpu as pltpu
from jax.sharding import PartitionSpec as P


LANES = 128
UNROLL = 4
F32 = jnp.float32
BF16 = jnp.bfloat16


def iota(shape, dim):
    return lax.broadcasted_iota(jnp.int32, shape, dim)


def standardize(values):
    average = jnp.mean(values, axis=-1, keepdims=True)
    centred = values - average
    return centred * lax.rsqrt(jnp.mean(centred * centred, axis=-1, keepdims=True) + 1e-05)


def dot(left, right, contract=(1, 0), precision=None):
    return lax.dot_general(
        left,
        right,
        (((contract[0],), (contract[1],)), ((), ())),
        preferred_element_type=F32,
        precision=precision,
    )


def tiling_matrix(rows, columns):
    return (iota((rows, columns), 1) % rows == iota((rows, columns), 0)).astype(BF16)


def call(body, outs, scratch=(), flops=0, data=0, far=0):
    near = pl.BlockSpec(memory_space=pltpu.VMEM)
    held = sum(
        math.prod(ref.shape) * jnp.dtype(ref.dtype).itemsize
        for ref in scratch
        if hasattr(ref, "shape") and ref.memory_space == pltpu.VMEM
    )

    def run(*operands):
        operands = [
            pltpu.with_memory_space_constraint(x, pltpu.HBM) if n < far else x
            for n, x in enumerate(operands)
        ]
        return pl.pallas_call(
            body,
            out_shape=outs,
            in_specs=[pl.BlockSpec(memory_space=pltpu.HBM)] * far + [near] * (len(operands) - far),
            out_specs=jax.tree.map(lambda _: near, outs),
            scratch_shapes=scratch,
            cost_estimate=pl.CostEstimate(flops=flops, bytes_accessed=data, transcendentals=0),
            compiler_params=pltpu.CompilerParams(vmem_limit_bytes=held * 5 // 4 + (4 << 20)),
        )(*operands)

    return run


def fetch(sources, targets, sems):
    copies = [
        pltpu.make_async_copy(source, target, sems.at[n])
        for n, (source, target) in enumerate(zip(sources, targets))
    ]
    for copy in copies:
        copy.start()
    return copies


def embed_kernel(
    ids_far,
    mask_far,
    profile_far,
    table_far,
    pair_far,
    msg_ref,
    arriving_ref,
    mask_ref,
    pair_ref,
    ids_ref,
    profile_ref,
    table_ref,
    padded,
    sems,
):
    copies = fetch(
        (ids_far, table_far, mask_far, profile_far, pair_far),
        (ids_ref, table_ref, mask_ref, profile_ref, pair_ref),
        sems,
    )
    sequences, residues, features = profile_ref.shape
    kinds = table_ref.shape[0]
    for copy in copies[:3]:
        copy.wait()
    padded[...] = jnp.zeros_like(padded)
    padded[0:kinds, :] = table_ref[...]
    columns = ids_ref[...].astype(F32).T
    labels = iota((residues, padded.shape[0]), 1).astype(F32)
    rows = sequences * residues
    mask = mask_ref[...].astype(F32).astype(BF16)
    msg_ref[rows:, :] = dot(mask, tiling_matrix(residues, features)).astype(BF16)
    table = padded[...]
    copies[3].wait()
    step = 4
    for start in range(0, sequences, step):
        hot = [
            (columns[:, s : s + 1] == labels).astype(F32).astype(BF16)
            for s in range(start, start + step)
        ]
        where = slice(start * residues, (start + step) * residues)
        profile = profile_ref[start : start + step].reshape(step * residues, features)
        arriving = profile.astype(F32) + dot(jnp.concatenate(hot, axis=0), table)
        arriving_ref[where, :] = arriving
        msg_ref[where, :] = standardize(arriving).astype(BF16)
    copies[4].wait()


def prepare_kernel(weights, *refs):
    far, pair_ref, refs = refs[:weights], refs[weights], refs[weights + 1 :]
    near, (out_ref, matrix_ref, sems) = refs[: weights - 1], refs[weights - 1 :]
    copies = fetch(far[-1:] + far[:-1], (matrix_ref,) + near, sems)
    rows, columns, width = pair_ref.shape
    copies[0].wait()
    matrix = matrix_ref[...]
    step = LANES // columns
    for start in range(0, rows, step):
        part = pair_ref[start : start + step].reshape(step * columns, width).astype(F32)
        out_ref[:, start * columns : (start + step) * columns] = dot(
            matrix, standardize(part), (1, 1), lax.Precision.HIGHEST
        )
    for copy in copies[1:]:
        copy.wait()


def block_kernel(mix_ref, block_ref, wide):
    width = other = math.isqrt(mix_ref.shape[0])
    pair_width = mix_ref.shape[1]
    fit = LANES // width
    wide[...] = mix_ref[...].astype(F32)
    blank = jnp.zeros((width, pair_width), BF16)
    for d in range(other):
        piece = wide[pl.ds(d, width, stride=other), :].astype(BF16)
        for p in range(fit):
            spot = slice((d * fit + p) * width, (d * fit + p + 1) * width)
            for q in range(fit):
                block_ref[spot, q * pair_width : (q + 1) * pair_width] = (
                    piece if q == p else blank
                )


def project_kernel(position, *refs):
    blocks = len(position)
    msgs = refs[:blocks]
    wq_ref, wk_ref, wv_ref, wg_ref, q_ref, k_ref, v_ref, g_ref, pen_ref = refs[blocks:]
    sequences, residues, _ = q_ref.shape
    rows = sequences * residues
    total = pen_ref.shape[1]
    x_own, c_own = lax.axis_index("gy"), lax.axis_index("gz")
    own = msgs[0][0:rows, :]
    q_ref[...] = dot(own, wq_ref[...]).astype(BF16).reshape(q_ref.shape)
    g_ref[...] = jax.nn.sigmoid(dot(own, wg_ref[...])).reshape(g_ref.shape)
    lane_block = iota((sequences, total), 1) // residues
    present = jnp.zeros((sequences, total), F32)
    for msg, (shift_y, shift_z, size_y, size_z) in zip(msgs, position):
        block = lax.rem(x_own - shift_y + size_y, size_y) * size_z + lax.rem(
            c_own - shift_z + size_z, size_z
        )
        where = pl.ds(pl.multiple_of(block * residues, residues), residues)
        normed = msg[0:rows, :]
        k_ref[:, where, :] = dot(normed, wk_ref[...]).astype(BF16).reshape(q_ref.shape)
        v_ref[:, where, :] = dot(normed, wv_ref[...]).astype(BF16).reshape(q_ref.shape)
        tiled = msg[rows : rows + sequences, :].astype(F32)
        while tiled.shape[1] < total:
            tiled = jnp.concatenate([tiled, tiled], axis=1)
        present = jnp.where(lane_block == block, tiled[:, 0:total], present)
    pen_ref[...] = (present - 1.0) * 1000000000.0


def attend_kernel(heads, groups, *refs):
    biases, refs = refs[:groups], refs[groups:]
    attend_body(heads, biases, *refs)


def attend_body(
    heads,
    biases,
    q_ref,
    k_ref,
    v_ref,
    g_ref,
    pen_ref,
    arriving_ref,
    mask_ref,
    wr_ref,
    wf_ref,
    ws_ref,
    profile_ref,
    left_ref,
    right_ref,
    bias_ref,
    spread,
    bias,
    scored,
    weighed,
    belows,
    gated,
    leftish,
    rightish,
):
    sequences, residues, features = q_ref.shape
    total = k_ref.shape[1]
    size = features // heads
    per = LANES // size
    fit = LANES // residues
    z_own = lax.axis_index("gx")
    for other, ref in enumerate(biases):
        bias_ref[z_own ^ other] = ref[...]
    lane = iota((heads, LANES), 1) // residues
    for i in range(residues):
        tile, inner = divmod(i, fit)
        for column in range(total // LANES):
            value = None
            for slot in range(fit):
                source = bias_ref[
                    column * fit + slot, :, tile * LANES : (tile + 1) * LANES
                ]
                shift = ((slot - inner) % fit) * residues
                if shift:
                    source = pltpu.roll(source, shift, 1)
                value = source if value is None else jnp.where(lane == slot, source, value)
            spread[column, i * heads : (i + 1) * heads, :] = value
    for column in range(total // LANES):
        for h in range(heads):
            bias[
                h * residues : (h + 1) * residues, column * LANES : (column + 1) * LANES
            ] = spread[column, pl.ds(h, residues, stride=heads), :]
    scale = size ** (-0.5)
    span = per * residues
    own_lanes = iota((span, LANES), 0) // residues == iota((span, LANES), 1) // size
    small_lanes = [iota((residues, LANES), 1) // size == p for p in range(per)]
    parts = [
        (slice(part * LANES, (part + 1) * LANES), slice(part * span, (part + 1) * span))
        for part in range(heads // per)
    ]

    def score(s, carry):
        penalty = pen_ref[pl.ds(s, 1), :]
        for lanes, span_rows in parts:
            query = q_ref[s, :, lanes]
            stacked = jnp.concatenate([query] * per, axis=0)
            stacked = jnp.where(own_lanes, stacked, jnp.zeros_like(stacked))
            scores = dot(stacked, k_ref[s, :, lanes], (1, 1)) * scale
            scored[s, span_rows, :] = scores + bias[span_rows, :] + penalty
        return carry

    def weigh(s, carry):
        for lanes, span_rows in parts:
            scores = scored[s, span_rows, :]
            top = jnp.max(scores, axis=1, keepdims=True)
            weights = jnp.exp(scores - top)
            aggregate = jnp.sum(weights, axis=1, keepdims=True)
            weighed[s, span_rows, :] = weights.astype(BF16)
            below = jnp.broadcast_to(aggregate[0:residues, :], (residues, LANES))
            for p in range(1, per):
                rows = slice(p * residues, (p + 1) * residues)
                below = jnp.where(small_lanes[p], aggregate[rows, :], below)
            belows[s, :, lanes] = g_ref[s, :, lanes] / below
        return carry

    def gather(s, carry):
        for lanes, span_rows in parts:
            mixed = dot(weighed[s, span_rows, :], v_ref[s, :, lanes])
            value = mixed[0:residues, :]
            for p in range(1, per):
                rows = slice(p * residues, (p + 1) * residues)
                value = jnp.where(small_lanes[p], mixed[rows, :], value)
            gated[s, :, lanes] = (belows[s, :, lanes] * value).astype(BF16)
        return carry

    for stage in (score, weigh, gather):
        lax.fori_loop(0, sequences, stage, 0, unroll=UNROLL)

    rows = sequences * residues
    refreshed = (
        arriving_ref[...] + dot(gated[...].reshape(rows, features), wr_ref[...])
    ).astype(BF16)
    profile_ref[...] = refreshed.reshape(profile_ref.shape)
    normed = standardize(refreshed.astype(F32)).astype(BF16)
    leftish[...] = dot(normed, jnp.concatenate([wf_ref[...]] * (LANES // wf_ref.shape[0])), (1, 1))
    width = ws_ref.shape[0]
    for s in range(sequences):
        piece = normed[s * residues : (s + 1) * residues, :]
        rightish[s * width : (s + 1) * width, :] = dot(
            ws_ref[...], jnp.concatenate([piece] * fit, axis=0), (1, 1)
        )
    mask = mask_ref[...].astype(F32).astype(BF16)
    wide = residues * width
    expand = (iota((residues, wide), 1) // width == iota((residues, wide), 0)).astype(BF16)
    left_mask = dot(mask, expand)
    right_mask = dot(mask, tiling_matrix(residues, width * residues))
    for tile in range(wide // LANES):
        lanes = slice(tile * LANES, (tile + 1) * LANES)
        for source, stride, step, target, present in (
            (leftish, residues, width, left_ref, left_mask),
            (rightish, width, residues, right_ref, right_mask),
        ):
            group = iota((sequences, LANES), 1) // step
            count = LANES // step
            value = source[pl.ds(tile * count, sequences, stride=stride), :]
            for p in range(1, count):
                other = source[pl.ds(tile * count + p, sequences, stride=stride), :]
                value = jnp.where(group == p, other, value)
            target[:, lanes] = (value * present[:, lanes]).astype(BF16)
    left_ref[:, wide:] = right_mask[:, 0:LANES].astype(BF16)
    right_ref[:, wide:] = right_mask[:, 0:LANES].astype(BF16)


def pair_kernel(left_from, right_from, *refs):
    lefts = refs[: len(left_from)]
    rights = refs[len(left_from) : len(left_from) + len(right_from)]
    (pair_ref, block_ref, w1_ref, w2_ref, out_ref, left, right, stacked, middle) = refs[
        len(left_from) + len(right_from) :
    ]
    sequences = lefts[0].shape[0]
    rows, columns, pair_width = pair_ref.shape
    z_own, x_own, c_own = (lax.axis_index(n) for n in ("gx", "gy", "gz"))
    for ref, other in zip(lefts, left_from):
        start = (z_own ^ other) * sequences
        left[pl.ds(pl.multiple_of(start, sequences), sequences), :] = ref[...]
    for ref, (shift_y, shift_z, size_y, size_z) in zip(rights, right_from):
        block = lax.rem(x_own - shift_y + size_y, size_y) * size_z + lax.rem(
            c_own - shift_z + size_z, size_z
        )
        right[pl.ds(pl.multiple_of(block * sequences, sequences), sequences), :] = ref[...]
    wide = left.shape[1] - LANES
    width = wide // rows
    fit = LANES // width
    depth = wide // columns
    count = dot(right[:, wide:], left[:, wide:], (0, 0))[0:columns, :]
    share = 1.0 / (count + 1.0)
    flipped = right[:, 0:wide].T
    tiles = wide // LANES
    pack = 2 if tiles % 2 == 0 else 1
    for start in range(0, tiles, pack):
        outer = dot(flipped, left[:, start * LANES : (start + pack) * LANES]).astype(BF16)
        for q in range(pack):
            for d in range(depth):
                stacked[
                    (start + q) * columns : (start + q + 1) * columns,
                    d * LANES : (d + 1) * LANES,
                ] = outer[d * columns : (d + 1) * columns, q * LANES : (q + 1) * LANES]
    mixed = dot(stacked[...], block_ref[...])
    for i in range(rows):
        tile, inner = divmod(i, fit)
        part = mixed[
            tile * columns : (tile + 1) * columns,
            inner * pair_width : (inner + 1) * pair_width,
        ]
        middle[i] = pair_ref[i].astype(F32) + part * share[:, i : i + 1]
    flat = middle[...].reshape(rows * columns, pair_width)
    normed = standardize(flat).astype(BF16)
    hidden = jnp.maximum(dot(normed, w1_ref[...]), 0.0).astype(BF16)
    out_ref[...] = (flat + dot(hidden, w2_ref[...])).astype(BF16).reshape(out_ref.shape)


def local(
    sizes,
    alignment_token_ids,
    homolog_profile,
    alignment_mask,
    pair_features,
    symbol_lookup_weights,
    asking_weights,
    lookup_weights,
    content_weights,
    sigmoid_switch_weights,
    resulting_weights,
    pair_bias_matrix,
    first_factor_weights,
    second_factor_weights,
    outer_mixing_weight,
    widening_weight,
    narrowing_weight,
):
    size_x, size_y, size_z = sizes
    sequences, residues, features = homolog_profile.shape
    heads = pair_bias_matrix.shape[1]
    width = first_factor_weights.shape[1]
    pair_rows, pair_columns, pair_width = pair_features.shape
    total = residues * size_y * size_z
    rows = sequences * residues
    shape = jax.ShapeDtypeStruct

    local_pair = shape(pair_features.shape, BF16)
    local_mask = shape(alignment_mask.shape, jnp.int32)
    msg, arriving, mask, pair = call(
        embed_kernel,
        (
            shape((rows + sequences, features), BF16),
            shape((rows, features), F32),
            local_mask,
            local_pair,
        ),
        [
            pltpu.VMEM(alignment_token_ids.shape, jnp.int32),
            pltpu.VMEM(homolog_profile.shape, BF16),
            pltpu.VMEM(symbol_lookup_weights.shape, BF16),
            pltpu.VMEM((LANES, features), BF16),
            pltpu.SemaphoreType.DMA((5,)),
        ],
        flops=2 * rows * LANES * features,
        data=rows * features * 8,
        far=5,
    )(
        alignment_token_ids,
        alignment_mask,
        homolog_profile,
        symbol_lookup_weights,
        pair_features,
    )

    def shift(value, axis, count, step):
        return lax.ppermute(value, axis, [(n, (n + step) % count) for n in range(count)])

    far = [msg] + [shift(msg, "gy", size_y, r) for r in range(1, size_y)]
    position, msgs = [], []
    for r in range(size_y):
        for t in range(size_z):
            position.append((r, t, size_y, size_z))
            msgs.append(far[r] if t == 0 else shift(far[r], "gz", size_z, t))

    fit = LANES // width
    weights = (
        asking_weights,
        lookup_weights,
        content_weights,
        sigmoid_switch_weights,
        resulting_weights,
        first_factor_weights.T,
        second_factor_weights.T,
        widening_weight,
        narrowing_weight,
        outer_mixing_weight,
    )
    wq, wk, wv, wg, wr, wf, ws, w1, w2, mix, bias_local = call(
        functools.partial(prepare_kernel, len(weights) + 1),
        tuple(shape(w.shape, w.dtype) for w in weights)
        + (shape((heads, pair_rows * pair_columns), F32),),
        [
            pltpu.VMEM(pair_bias_matrix.T.shape, F32),
            pltpu.SemaphoreType.DMA((len(weights) + 1,)),
        ],
        flops=2 * 6 * pair_rows * pair_columns * pair_width * LANES,
        data=pair_rows * pair_columns * pair_width * 2,
        far=len(weights) + 1,
    )(*weights, pair_bias_matrix.T, pair)
    biases = [bias_local] + [
        lax.ppermute(bias_local, "gx", [(n, n ^ m) for n in range(size_x)])
        for m in range(1, size_x)
    ]

    three = (sequences, residues, features)
    keys = (sequences, total, features)
    queries, keys, values, gates, penalty = call(
        functools.partial(project_kernel, tuple(position)),
        (
            shape(three, BF16),
            shape(keys, BF16),
            shape(keys, BF16),
            shape(three, F32),
            shape((sequences, total), F32),
        ),
        flops=2 * sequences * (total + residues) * features * features * 2,
        data=sequences * total * features * 6,
    )(*msgs, wq, wk, wv, wg)

    wide = residues * width
    message = shape((sequences, wide + LANES), BF16)
    refreshed, left_own, right_own = call(
        functools.partial(attend_kernel, heads, size_x),
        (shape(three, BF16), message, message),
        [
            pltpu.VMEM((size_x, heads, pair_rows * pair_columns), F32),
            pltpu.VMEM((total // LANES, residues * heads, LANES), F32),
            pltpu.VMEM((heads * residues, total), F32),
            pltpu.VMEM((sequences, heads * residues, total), F32),
            pltpu.VMEM((sequences, heads * residues, total), BF16),
            pltpu.VMEM(three, F32),
            pltpu.VMEM(three, BF16),
            pltpu.VMEM((rows, LANES), F32),
            pltpu.VMEM((sequences * width, LANES), F32),
        ],
        flops=4 * sequences * heads * residues * total * LANES,
        data=sequences * total * features * 4,
    )(*biases, queries, keys, values, gates, penalty, arriving, mask, wr, wf, ws)

    lefts = [left_own] + [
        lax.ppermute(left_own, "gx", [(n, n ^ m) for n in range(size_x)])
        for m in range(1, size_x)
    ]
    right_from, rights = [], []
    blocks = size_y * size_z
    for r in range(size_y):
        pairs = []
        for a in range(size_x):
            for b in range(blocks):
                to = ((a // size_z + r) % size_y) * size_z + a % size_z
                pairs.append((a * blocks + b, b * blocks + to))
        got = lax.ppermute(right_own, ("gx", "gy", "gz"), pairs)
        for t in range(size_z):
            right_from.append((r, t, size_y, size_z))
            rights.append(got if t == 0 else shift(got, "gz", size_z, t))

    block = call(
        block_kernel,
        shape((width * width * fit, pair_width * fit), BF16),
        [pltpu.VMEM(outer_mixing_weight.shape, F32)],
        data=width * width * fit * pair_width * fit * 2,
    )(mix)

    depth = sequences * size_x
    pair_output = call(
        functools.partial(pair_kernel, tuple(range(size_x)), tuple(right_from)),
        shape(pair_features.shape, BF16),
        [
            pltpu.VMEM((depth, wide + LANES), BF16),
            pltpu.VMEM((depth, wide + LANES), BF16),
            pltpu.VMEM((pair_rows // fit * pair_columns, width * LANES), BF16),
            pltpu.VMEM(pair_features.shape, F32),
        ],
        flops=2 * pair_rows * pair_columns * width * width * pair_width * fit,
        data=width * width * fit * pair_width * fit * 2,
    )(*lefts, *rights, pair, block, w1, w2)
    return refreshed, pair_output


def solution(mesh):
    sizes = tuple(mesh.shape[name] for name in ("gx", "gy", "gz"))
    assert sizes[0] == sizes[1] * sizes[2] and sizes[0] & (sizes[0] - 1) == 0
    in_specs = (
        P(("grp", "gx"), ("gy", "gz")),
        P(("grp", "gx"), ("gy", "gz"), None),
        P(("grp", "gx"), ("gy", "gz")),
        P(("grp", "gy", "gz"), "gx", None),
    ) + (P(),) * 12
    out_specs = (P(("grp", "gx"), ("gy", "gz"), None), P(("grp", "gy", "gz"), "gx", None))

    def body(*args):
        return local(sizes, *args)

    return jax.shard_map(
        body, mesh=mesh, in_specs=in_specs, out_specs=out_specs, check_vma=False
    )
```

```python
import functools
import math

import jax
import jax.numpy as jnp
from jax import lax
from jax.experimental import pallas as pl
from jax.experimental.pallas import tpu as pltpu
from jax.sharding import PartitionSpec as P


LANES = 128
LAG = 4
SKEW = 4
SKEW_SMALL = 1
F32 = jnp.float32
BF16 = jnp.bfloat16


def iota(shape, dim):
    return lax.broadcasted_iota(jnp.int32, shape, dim)


def standardize(values):
    average = jnp.mean(values, axis=-1, keepdims=True)
    centred = values - average
    return centred * lax.rsqrt(jnp.mean(centred * centred, axis=-1, keepdims=True) + 1e-05)


def dot(left, right, contract=(1, 0), precision=None):
    return lax.dot_general(
        left,
        right,
        (((contract[0],), (contract[1],)), ((), ())),
        preferred_element_type=F32,
        precision=precision,
    )


def tiling_matrix(rows, columns):
    return (iota((rows, columns), 1) % rows == iota((rows, columns), 0)).astype(BF16)


def call(body, outs, scratch=(), flops=0, data=0, far=0, aliases={}):
    near = pl.BlockSpec(memory_space=pltpu.VMEM)
    held = sum(
        math.prod(ref.shape) * jnp.dtype(ref.dtype).itemsize
        for ref in scratch
        if hasattr(ref, "shape") and ref.memory_space == pltpu.VMEM
    )

    def run(*operands):
        operands = [
            pltpu.with_memory_space_constraint(x, pltpu.HBM) if n < far else x
            for n, x in enumerate(operands)
        ]
        return pl.pallas_call(
            body,
            out_shape=outs,
            in_specs=[pl.BlockSpec(memory_space=pltpu.HBM)] * far + [near] * (len(operands) - far),
            out_specs=jax.tree.map(lambda _: near, outs),
            scratch_shapes=scratch,
            cost_estimate=pl.CostEstimate(flops=flops, bytes_accessed=data, transcendentals=0),
            compiler_params=pltpu.CompilerParams(vmem_limit_bytes=held * 5 // 4 + (6 << 20)),
            input_output_aliases=aliases,
        )(*operands)

    return run


def fetch(sources, targets, sems):
    copies = [
        pltpu.make_async_copy(source, target, sems.at[n])
        for n, (source, target) in enumerate(zip(sources, targets))
    ]
    for copy in copies:
        copy.start()
    return copies


def embed_kernel(
    ids_far,
    mask_far,
    profile_far,
    table_far,
    pair_far,
    matrix_far,
    msg_ref,
    arriving_ref,
    mask_ref,
    pair_ref,
    matrix_ref,
    ids_ref,
    profile_ref,
    table_ref,
    padded,
    sems,
):
    copies = fetch(
        (ids_far, table_far, mask_far, profile_far, pair_far, matrix_far),
        (ids_ref, table_ref, mask_ref, profile_ref, pair_ref, matrix_ref),
        sems,
    )
    sequences, residues, features = profile_ref.shape
    kinds = table_ref.shape[0]
    for copy in copies[:3]:
        copy.wait()
    padded[...] = jnp.zeros_like(padded)
    padded[0:kinds, :] = table_ref[...]
    columns = ids_ref[...].astype(F32).T
    labels = iota((residues, padded.shape[0]), 1).astype(F32)
    rows = sequences * residues
    mask = mask_ref[...].astype(F32).astype(BF16)
    msg_ref[rows:, :] = dot(mask, tiling_matrix(residues, features)).astype(BF16)
    table = padded[...]
    copies[3].wait()
    step = 4
    for start in range(0, sequences, step):
        hot = [
            (columns[:, s : s + 1] == labels).astype(F32).astype(BF16)
            for s in range(start, start + step)
        ]
        where = slice(start * residues, (start + step) * residues)
        profile = profile_ref[start : start + step].reshape(step * residues, features)
        arriving = profile.astype(F32) + dot(jnp.concatenate(hot, axis=0), table)
        arriving_ref[where, :] = arriving
        msg_ref[where, :] = standardize(arriving).astype(BF16)
    for copy in copies[4:]:
        copy.wait()


def prepare_kernel(weights, *refs):
    far, (pair_ref, matrix_ref), refs = refs[:weights], refs[weights : weights + 2], refs[weights + 2 :]
    near, (out_ref, sems) = refs[:weights], refs[weights:]
    copies = fetch(far, near, sems)
    rows, columns, width = pair_ref.shape
    matrix = matrix_ref[...]
    step = LANES // columns
    for start in range(0, rows, step):
        part = pair_ref[start : start + step].reshape(step * columns, width).astype(F32)
        bias = dot(matrix, standardize(part), (1, 1), lax.Precision.HIGHEST)
        out_ref[:, start * columns : (start + step) * columns] = bias
    for copy in copies:
        copy.wait()


def block_kernel(mix_ref, block_ref, wide):
    turns = block_ref.shape[0]
    width = other = math.isqrt(mix_ref.shape[0])
    pitch = wide.shape[0] // width
    for c in range(width):
        wide[c * pitch : c * pitch + other, :] = mix_ref[c * other : (c + 1) * other, :].astype(F32)
    for d in range(other):
        piece = wide[pl.ds(d, width, stride=pitch), :].astype(BF16)
        high, low = divmod(d, turns)
        for turn in range(turns):
            spot = (high * turns + (low + turn) % turns) * width
            block_ref[turn, spot : spot + width, :] = piece


def block_rows(shift, residues):
    shift_y, shift_z, size_y, size_z = shift
    block = lax.rem(lax.axis_index("gy") - shift_y + size_y, size_y) * size_z + lax.rem(
        lax.axis_index("gz") - shift_z + size_z, size_z
    )
    return block, pl.ds(pl.multiple_of(block * residues, residues), residues)


def project_kernel(position, *refs):
    msgs = refs[: len(position)]
    wq_ref, wk_ref, wv_ref, wg_ref, q_ref, k_ref, v_ref, g_ref = refs[len(position) :]
    sequences, residues, _ = q_ref.shape
    rows = sequences * residues
    for msg, place in zip(msgs, position):
        _, where = block_rows(place, residues)
        normed = msg[0:rows, :]
        k_ref[:, where, :] = dot(normed, wk_ref[...]).astype(BF16).reshape(q_ref.shape)
        v_ref[:, where, :] = dot(normed, wv_ref[...]).astype(BF16).reshape(q_ref.shape)
    own = msgs[0][0:rows, :]
    q_ref[...] = dot(own, wq_ref[...]).astype(BF16).reshape(q_ref.shape)
    g_ref[...] = jax.nn.sigmoid(dot(own, wg_ref[...])).reshape(g_ref.shape)


def score_kernel(heads, position, late, *refs):
    msgs = refs[: len(position)]
    q_ref, _, _, wk_ref, wv_ref, k_ref, v_ref, scored, pen_ref = refs[len(position) :]
    sequences, residues, features = q_ref.shape
    rows = sequences * residues
    total = pen_ref.shape[1]
    lane_block = iota((sequences, total), 1) // residues
    present = jnp.zeros((sequences, total), F32)
    for n, (msg, place) in enumerate(zip(msgs, position)):
        block, where = block_rows(place, residues)
        if n in late:
            normed = msg[0:rows, :]
            k_ref[:, where, :] = dot(normed, wk_ref[...]).astype(BF16).reshape(q_ref.shape)
            v_ref[:, where, :] = dot(normed, wv_ref[...]).astype(BF16).reshape(q_ref.shape)
        tiled = msg[rows : rows + sequences, :].astype(F32)
        while tiled.shape[1] < total:
            tiled = jnp.concatenate([tiled, tiled], axis=1)
        present = jnp.where(lane_block == block, tiled[:, 0:total], present)
    pen_ref[...] = (present - 1.0) * 1000000000.0
    size = features // heads
    per = LANES // size
    span = per * residues
    scale = size ** (-0.5)
    own_lanes = iota((span, LANES), 0) // residues == iota((span, LANES), 1) // size
    for s in range(sequences):
        for part in range(heads // per):
            lanes = slice(part * LANES, (part + 1) * LANES)
            stacked = jnp.concatenate([q_ref[s, :, lanes]] * per, axis=0)
            stacked = jnp.where(own_lanes, stacked, jnp.zeros_like(stacked))
            scored[s, part * span : (part + 1) * span, :] = (
                dot(stacked, k_ref[s, :, lanes], (1, 1)) * scale
            )


def attend_kernel(heads, groups, *refs):
    attend_body(heads, refs[:groups], *refs[groups:])


def attend_body(
    heads,
    biases,
    scored,
    v_ref,
    g_ref,
    pen_ref,
    arriving_ref,
    mask_ref,
    wr_ref,
    wf_ref,
    ws_ref,
    profile_ref,
    left_ref,
    right_ref,
    bias_ref,
    spread,
    bias,
    weighed,
    gated,
    leftish,
    rightish,
):
    sequences, residues, features = g_ref.shape
    total = v_ref.shape[1]
    size = features // heads
    per = LANES // size
    fit = LANES // residues
    pitch = spread.shape[1] // residues
    z_own = lax.axis_index("gx")
    for other, ref in enumerate(biases):
        bias_ref[z_own ^ other] = ref[...]
    lane = iota((heads, LANES), 1) // residues
    for i in range(residues):
        tile, inner = divmod(i, fit)
        for column in range(total // LANES):
            value = None
            for slot in range(fit):
                source = bias_ref[
                    column * fit + slot, :, tile * LANES : (tile + 1) * LANES
                ]
                shift = ((slot - inner) % fit) * residues
                if shift:
                    source = pltpu.roll(source, shift, 1)
                value = source if value is None else jnp.where(lane == slot, source, value)
            spread[column, i * pitch : i * pitch + heads, :] = value
    for column in range(total // LANES):
        for h in range(heads):
            bias[
                h * residues : (h + 1) * residues, column * LANES : (column + 1) * LANES
            ] = spread[column, pl.ds(h, residues, stride=pitch), :]
    span = per * residues
    small_lanes = [iota((residues, LANES), 1) // size == p for p in range(per)]
    parts = [
        (slice(part * LANES, (part + 1) * LANES), slice(part * span, (part + 1) * span))
        for part in range(heads // per)
    ]
    ones = jnp.ones((total, LANES), BF16)

    def weigh(s):
        penalty = pen_ref[s : s + 1, :]
        for lanes, span_rows in parts:
            scores = scored[s, span_rows, :] + bias[span_rows, :] + penalty
            top = jnp.max(scores, axis=1, keepdims=True)
            weighed[s, span_rows, :] = jnp.exp(scores - top).astype(BF16)

    def gather(s):
        for lanes, span_rows in parts:
            mixed = dot(
                weighed[s, span_rows, :], jnp.concatenate([v_ref[s, :, lanes], ones], axis=1)
            )
            value = mixed[0:residues, :]
            for p in range(1, per):
                rows = slice(p * residues, (p + 1) * residues)
                mask = jnp.concatenate([small_lanes[p], small_lanes[p]], axis=1)
                value = jnp.where(mask, mixed[rows, :], value)
            gated[s, :, lanes] = (
                g_ref[s, :, lanes] * (value[:, :LANES] / value[:, LANES:])
            ).astype(BF16)

    for step in range(sequences + LAG):
        if step < sequences:
            weigh(step)
        if step >= LAG:
            gather(step - LAG)

    rows = sequences * residues
    refreshed = (
        arriving_ref[...] + dot(gated[...].reshape(rows, features), wr_ref[...])
    ).astype(BF16)
    profile_ref[...] = refreshed.reshape(profile_ref.shape)
    normed = standardize(refreshed.astype(F32)).astype(BF16)
    width = ws_ref.shape[0]
    left_pitch, right_pitch = leftish.shape[0] // sequences, rightish.shape[0] // sequences
    sides = dot(normed, jnp.concatenate([wf_ref[...]] * (LANES // width)), (1, 1))
    for s in range(sequences):
        piece = normed[s * residues : (s + 1) * residues, :]
        leftish[s * left_pitch : s * left_pitch + residues, :] = sides[
            s * residues : (s + 1) * residues, :
        ]
        rightish[s * right_pitch : s * right_pitch + width, :] = dot(
            ws_ref[...], jnp.concatenate([piece] * fit, axis=0), (1, 1)
        )
    mask = mask_ref[...].astype(F32).astype(BF16)
    wide = residues * width
    expand = (iota((residues, wide), 1) // width == iota((residues, wide), 0)).astype(BF16)
    left_mask = dot(mask, expand)
    right_mask = dot(mask, tiling_matrix(residues, LANES))
    turns = LANES // width
    high = width // turns
    left_order = list(range(residues))
    right_order = [h * turns + low for low in range(turns) for h in range(high)]
    for tile in range(wide // LANES):
        lanes = slice(tile * LANES, (tile + 1) * LANES)
        for source, pitch, step, order, target, present in (
            (leftish, left_pitch, width, left_order, left_ref, left_mask[:, lanes]),
            (rightish, right_pitch, residues, right_order, right_ref, right_mask),
        ):
            group = iota((sequences, LANES), 1) // step
            count = LANES // step
            value = None
            for p in range(count):
                other = source[pl.ds(order[tile * count + p], sequences, stride=pitch), :]
                value = other if p == 0 else jnp.where(group == p, other, value)
            target[:, lanes] = (value * present).astype(BF16)
    left_ref[:, wide:] = right_mask.astype(BF16)
    right_ref[:, wide:] = right_mask.astype(BF16)


def pair_kernel(left_from, right_from, *refs):
    lefts = refs[: len(left_from)]
    rights = refs[len(left_from) : len(left_from) + len(right_from)]
    (pair_ref, block_ref, w1_ref, w2_ref, out_ref, left, right, flipped, spread, stacked, middle, normed) = refs[
        len(left_from) + len(right_from) :
    ]
    sequences = lefts[0].shape[0]
    rows, columns, _ = pair_ref.shape
    z_own, x_own, c_own = (lax.axis_index(n) for n in ("gx", "gy", "gz"))
    for ref, other in zip(lefts, left_from):
        start = (z_own ^ other) * sequences
        left[pl.ds(pl.multiple_of(start, sequences), sequences), :] = ref[...]
    for ref, (shift_y, shift_z, size_y, size_z) in zip(rights, right_from):
        block = lax.rem(x_own - shift_y + size_y, size_y) * size_z + lax.rem(
            c_own - shift_z + size_z, size_z
        )
        right[pl.ds(pl.multiple_of(block * sequences, sequences), sequences), :] = ref[...]
    wide = left.shape[1] - LANES
    width = wide // rows
    fit = LANES // width
    high = wide // columns // fit
    count = dot(right[:, wide:], left[:, wide:], (0, 0))[0:columns, :]
    share = 1.0 / (count + 1.0)
    tiles = wide // LANES
    deep = left.shape[0]
    span = high * columns
    flipped[...] = jnp.concatenate(
        [right[:, low * span : (low + 1) * span] for low in range(fit)]
    ).T
    group = iota((deep, LANES), 1) // width
    for tile in range(tiles):
        lanes = slice(tile * LANES, (tile + 1) * LANES)
        chunk = left[:, lanes].astype(F32)
        for low in range(fit):
            rolled = pltpu.roll(chunk, low * width, 1) if low else chunk
            for turn in range(fit):
                spread[turn, low * deep : (low + 1) * deep, lanes] = jnp.where(
                    group == (low + turn) % fit, rolled, 0.0
                ).astype(BF16)

    def outer(turn):
        value = dot(flipped[...], spread[turn]).astype(BF16)
        for tile in range(tiles):
            for h in range(high):
                stacked[
                    turn, tile * columns : (tile + 1) * columns, h * LANES : (h + 1) * LANES
                ] = value[h * columns : (h + 1) * columns, tile * LANES : (tile + 1) * LANES]

    def mix(turn):
        mixed = dot(stacked[turn], block_ref[turn])
        for tile in range(tiles):
            i = tile * fit + turn
            where = slice(tile * columns, (tile + 1) * columns)
            middle[turn, where, :] = pair_ref[i].astype(F32) + mixed[where, :] * share[:, i : i + 1]

    def norm(turn):
        normed[turn] = standardize(middle[turn]).astype(BF16)

    def transition(turn):
        hidden = jnp.maximum(dot(normed[turn], w1_ref[...]), 0.0).astype(BF16)
        done = (middle[turn] + dot(hidden, w2_ref[...])).astype(BF16)
        for tile in range(tiles):
            out_ref[tile * fit + turn] = done[tile * columns : (tile + 1) * columns, :]

    stages = (outer, mix, norm, transition)
    for step in range(fit + len(stages) - 1):
        for late, stage in reversed(list(enumerate(stages))):
            if 0 <= step - late < fit:
                stage(step - late)


def local(
    sizes,
    alignment_token_ids,
    homolog_profile,
    alignment_mask,
    pair_features,
    symbol_lookup_weights,
    asking_weights,
    lookup_weights,
    content_weights,
    sigmoid_switch_weights,
    resulting_weights,
    pair_bias_matrix,
    first_factor_weights,
    second_factor_weights,
    outer_mixing_weight,
    widening_weight,
    narrowing_weight,
):
    size_x, size_y, size_z = sizes
    sequences, residues, features = homolog_profile.shape
    heads = pair_bias_matrix.shape[1]
    width = first_factor_weights.shape[1]
    pair_rows, pair_columns, pair_width = pair_features.shape
    total = residues * size_y * size_z
    rows = sequences * residues
    shape = jax.ShapeDtypeStruct

    local_pair = shape(pair_features.shape, BF16)
    local_mask = shape(alignment_mask.shape, jnp.int32)
    matrix_far = pair_bias_matrix.T
    msg, arriving, mask, pair, matrix = call(
        embed_kernel,
        (
            shape((rows + sequences, features), BF16),
            shape((rows, features), F32),
            local_mask,
            local_pair,
            shape(matrix_far.shape, F32),
        ),
        [
            pltpu.VMEM(alignment_token_ids.shape, jnp.int32),
            pltpu.VMEM(homolog_profile.shape, BF16),
            pltpu.VMEM(symbol_lookup_weights.shape, BF16),
            pltpu.VMEM((LANES, features), BF16),
            pltpu.SemaphoreType.DMA((6,)),
        ],
        flops=2 * rows * LANES * features,
        data=rows * features * 8,
        far=6,
    )(
        alignment_token_ids,
        alignment_mask,
        homolog_profile,
        symbol_lookup_weights,
        pair_features,
        matrix_far,
    )

    def shift(value, axis, count, step):
        return lax.ppermute(value, axis, [(n, (n + step) % count) for n in range(count)])

    far = [msg] + [shift(msg, "gy", size_y, r) for r in range(1, size_y)]
    position, msgs = [], []
    for r in range(size_y):
        for t in range(size_z):
            position.append((r, t, size_y, size_z))
            msgs.append(far[r] if t == 0 else shift(far[r], "gz", size_z, t))

    fit = LANES // width
    weights = (
        asking_weights,
        lookup_weights,
        content_weights,
        sigmoid_switch_weights,
        resulting_weights,
        first_factor_weights.T,
        second_factor_weights.T,
        widening_weight,
        narrowing_weight,
        outer_mixing_weight,
    )
    wq, wk, wv, wg, wr, wf, ws, w1, w2, mix, bias_local = call(
        functools.partial(prepare_kernel, len(weights)),
        tuple(shape(w.shape, w.dtype) for w in weights)
        + (shape((heads, pair_rows * pair_columns), F32),),
        [pltpu.SemaphoreType.DMA((len(weights),))],
        flops=2 * 6 * pair_rows * pair_columns * pair_width * LANES,
        data=pair_rows * pair_columns * pair_width * 2,
        far=len(weights),
    )(*weights, pair, matrix)
    biases = [bias_local]
    for m in range(1, size_x):
        biases.append(lax.ppermute(bias_local, "gx", [(n, n ^ m) for n in range(size_x)]))

    three = (sequences, residues, features)
    keys = (sequences, total, features)
    scores = (sequences, heads * residues, total)
    late = tuple(n for n, (r, t, _, _) in enumerate(position) if r and t)
    early = tuple(n for n in range(len(position)) if n not in late)
    queries, keys_early, values_early, gates = call(
        functools.partial(project_kernel, tuple(position[n] for n in early)),
        (shape(three, BF16), shape(keys, BF16), shape(keys, BF16), shape(three, F32)),
        flops=2 * rows * features * features * 2 * (len(early) + 1),
        data=sequences * total * features * 6,
    )(*(msgs[n] for n in early), wq, wk, wv, wg)
    _, values, scored, penalty = call(
        functools.partial(score_kernel, heads, tuple(position), late),
        (
            shape(keys, BF16),
            shape(keys, BF16),
            shape(scores, F32),
            shape((sequences, total), F32),
        ),
        flops=2 * rows * features * features * 2 * len(late),
        data=sequences * total * features * 6,
        aliases={len(msgs) + 1: 0, len(msgs) + 2: 1},
    )(*msgs, queries, keys_early, values_early, wk, wv)

    wide = residues * width
    message = shape((sequences, wide + LANES), BF16)
    refreshed, left_own, right_own = call(
        functools.partial(attend_kernel, heads, size_x),
        (shape(three, BF16), message, message),
        [
            pltpu.VMEM((size_x, heads, pair_rows * pair_columns), F32),
            pltpu.VMEM((total // LANES, residues * (heads + SKEW_SMALL), LANES), F32),
            pltpu.VMEM(scores[1:], F32),
            pltpu.VMEM(scores, BF16),
            pltpu.VMEM(three, BF16),
            pltpu.VMEM((sequences * (residues + SKEW), LANES), F32),
            pltpu.VMEM((sequences * (width + SKEW), LANES), F32),
        ],
        flops=4 * sequences * heads * residues * total * LANES,
        data=sequences * total * features * 4,
    )(*biases, scored, values, gates, penalty, arriving, mask, wr, wf, ws)

    lefts = [left_own]
    for m in range(1, size_x):
        lefts.append(lax.ppermute(left_own, "gx", [(n, n ^ m) for n in range(size_x)]))
    right_from, rights = [], []
    blocks = size_y * size_z
    for r in range(size_y):
        pairs = []
        for a in range(size_x):
            for b in range(blocks):
                to = ((a // size_z + r) % size_y) * size_z + a % size_z
                pairs.append((a * blocks + b, b * blocks + to))
        got = lax.ppermute(right_own, ("gx", "gy", "gz"), pairs)
        for t in range(size_z):
            right_from.append((r, t, size_y, size_z))
            rights.append(got if t == 0 else shift(got, "gz", size_z, t))

    block = call(
        block_kernel,
        shape((fit, width * width, pair_width), BF16),
        [pltpu.VMEM((width * (width + SKEW), pair_width), F32)],
        data=width * width * fit * pair_width * 2,
    )(mix)

    depth = sequences * size_x
    pair_output = call(
        functools.partial(pair_kernel, tuple(range(size_x)), tuple(right_from)),
        shape(pair_features.shape, BF16),
        [
            pltpu.VMEM((depth, wide + LANES), BF16),
            pltpu.VMEM((depth, wide + LANES), BF16),
            pltpu.VMEM((width // fit * pair_columns, fit * depth), BF16),
            pltpu.VMEM((fit, fit * depth, wide), BF16),
            pltpu.VMEM((fit, pair_rows // fit * pair_columns, width * width), BF16),
            pltpu.VMEM((fit, pair_rows // fit * pair_columns, pair_width), F32),
            pltpu.VMEM((fit, pair_rows // fit * pair_columns, pair_width), BF16),
        ],
        flops=2 * pair_rows * pair_columns * width * width * pair_width * fit,
        data=width * width * fit * pair_width * fit * 2,
    )(*lefts, *rights, pair, block, w1, w2)
    return refreshed, pair_output


def solution(mesh):
    sizes = tuple(mesh.shape[name] for name in ("gx", "gy", "gz"))
    assert sizes[0] == sizes[1] * sizes[2] and sizes[0] & (sizes[0] - 1) == 0
    in_specs = (
        P(("grp", "gx"), ("gy", "gz")),
        P(("grp", "gx"), ("gy", "gz"), None),
        P(("grp", "gx"), ("gy", "gz")),
        P(("grp", "gy", "gz"), "gx", None),
    ) + (P(),) * 12
    out_specs = (P(("grp", "gx"), ("gy", "gz"), None), P(("grp", "gy", "gz"), "gx", None))

    def body(*args):
        return local(sizes, *args)

    return jax.shard_map(
        body, mesh=mesh, in_specs=in_specs, out_specs=out_specs, check_vma=False
    )
```

```python
import functools
import math

import jax
import jax.numpy as jnp
from jax import lax
from jax.experimental import pallas as pl
from jax.experimental.pallas import tpu as pltpu
from jax.sharding import PartitionSpec as P


LANES = 128
LAG = 4
SKEW = 4
SKEW_SMALL = 1
F32 = jnp.float32
BF16 = jnp.bfloat16


def iota(shape, dim):
    return lax.broadcasted_iota(jnp.int32, shape, dim)


def standardize(values):
    average = jnp.mean(values, axis=-1, keepdims=True)
    centred = values - average
    return centred * lax.rsqrt(jnp.mean(centred * centred, axis=-1, keepdims=True) + 1e-05)


def dot(left, right, contract=(1, 0), precision=None):
    return lax.dot_general(
        left,
        right,
        (((contract[0],), (contract[1],)), ((), ())),
        preferred_element_type=F32,
        precision=precision,
    )


def tiling_matrix(rows, columns):
    return (iota((rows, columns), 1) % rows == iota((rows, columns), 0)).astype(BF16)


def call(body, outs, scratch=(), flops=0, data=0, far=0, aliases={}, sent=()):
    near = pl.BlockSpec(memory_space=pltpu.VMEM)
    held = sum(
        math.prod(ref.shape) * jnp.dtype(ref.dtype).itemsize
        for ref in scratch
        if hasattr(ref, "shape") and ref.memory_space == pltpu.VMEM
    )

    def run(*operands):
        operands = [
            pltpu.with_memory_space_constraint(x, pltpu.HBM) if n < far else x
            for n, x in enumerate(operands)
        ]
        return pl.pallas_call(
            body,
            out_shape=outs,
            in_specs=[pl.BlockSpec(memory_space=pltpu.HBM)] * far + [near] * (len(operands) - far),
            out_specs=[
                pl.BlockSpec(memory_space=pltpu.HBM) if n in sent else near
                for n in range(len(outs))
            ],
            scratch_shapes=scratch,
            cost_estimate=pl.CostEstimate(flops=flops, bytes_accessed=data, transcendentals=0),
            compiler_params=pltpu.CompilerParams(vmem_limit_bytes=held * 5 // 4 + (6 << 20)),
            input_output_aliases=aliases,
        )(*operands)

    return run


def fetch(sources, targets, sems):
    copies = [
        pltpu.make_async_copy(source, target, sems.at[n])
        for n, (source, target) in enumerate(zip(sources, targets))
    ]
    for copy in copies:
        copy.start()
    return copies


def embed_kernel(
    ids_far,
    mask_far,
    profile_far,
    table_far,
    pair_far,
    matrix_far,
    msg_ref,
    arriving_ref,
    mask_ref,
    pair_ref,
    matrix_ref,
    ids_ref,
    profile_ref,
    table_ref,
    padded,
    sems,
):
    copies = fetch(
        (ids_far, table_far, mask_far, profile_far, pair_far, matrix_far),
        (ids_ref, table_ref, mask_ref, profile_ref, pair_ref, matrix_ref),
        sems,
    )
    sequences, residues, features = profile_ref.shape
    kinds = table_ref.shape[0]
    for copy in copies[:3]:
        copy.wait()
    padded[...] = jnp.zeros_like(padded)
    padded[0:kinds, :] = table_ref[...]
    columns = ids_ref[...].astype(F32).T
    labels = iota((residues, padded.shape[0]), 1).astype(F32)
    rows = sequences * residues
    mask = mask_ref[...].astype(F32).astype(BF16)
    msg_ref[rows:, :] = dot(mask, tiling_matrix(residues, features)).astype(BF16)
    table = padded[...]
    copies[3].wait()
    step = 4
    for start in range(0, sequences, step):
        hot = [
            (columns[:, s : s + 1] == labels).astype(F32).astype(BF16)
            for s in range(start, start + step)
        ]
        where = slice(start * residues, (start + step) * residues)
        profile = profile_ref[start : start + step].reshape(step * residues, features)
        arriving = profile.astype(F32) + dot(jnp.concatenate(hot, axis=0), table)
        arriving_ref[where, :] = arriving
        msg_ref[where, :] = standardize(arriving).astype(BF16)
    for copy in copies[4:]:
        copy.wait()


def thirds(values):
    high = values.astype(BF16)
    rest = values - high.astype(F32)
    middle = rest.astype(BF16)
    return [high, middle, (rest - middle.astype(F32)).astype(BF16)]


def prepare_kernel(weights, *refs):
    far, (pair_ref, matrix_ref), refs = refs[:weights], refs[weights : weights + 2], refs[weights + 2 :]
    near, (out_ref, sems) = refs[:weights], refs[weights:]
    copies = fetch(far, near, sems)
    rows, columns, width = pair_ref.shape
    matrix = thirds(matrix_ref[...])
    stacked = jnp.concatenate([jnp.concatenate(matrix, axis=0)] * len(matrix), axis=1)
    heads = matrix_ref.shape[0]
    step = LANES // columns
    for start in range(0, rows, step):
        part = pair_ref[start : start + step].reshape(step * columns, width).astype(F32)
        products = dot(stacked, jnp.concatenate(thirds(standardize(part)), axis=1), (1, 1))
        bias = products[2 * heads :] + products[heads : 2 * heads] + products[:heads]
        out_ref[:, start * columns : (start + step) * columns] = bias
    for copy in copies:
        copy.wait()


def block_kernel(
    mix_far, w1_far, w2_far, profile_ref, block_ref, w1_ref, w2_ref, profile_far, mix_ref, wide, sems
):
    copies = fetch(
        (mix_far, w1_far, w2_far, profile_ref), (mix_ref, w1_ref, w2_ref, profile_far), sems
    )
    copies[0].wait()
    turns = block_ref.shape[0]
    width = other = math.isqrt(mix_ref.shape[0])
    pitch = wide.shape[0] // width
    for c in range(width):
        wide[c * pitch : c * pitch + other, :] = mix_ref[c * other : (c + 1) * other, :].astype(F32)
    for d in range(other):
        piece = wide[pl.ds(d, width, stride=pitch), :].astype(BF16)
        high, low = divmod(d, turns)
        for turn in range(turns):
            spot = (high * turns + (low + turn) % turns) * width
            block_ref[turn, spot : spot + width, :] = piece
    for copy in copies[1:]:
        copy.wait()


def block_rows(shift, residues):
    shift_y, shift_z, size_y, size_z = shift
    block = lax.rem(lax.axis_index("gy") - shift_y + size_y, size_y) * size_z + lax.rem(
        lax.axis_index("gz") - shift_z + size_z, size_z
    )
    return block, pl.ds(pl.multiple_of(block * residues, residues), residues)


def project_kernel(position, *refs):
    msgs = refs[: len(position)]
    wq_ref, wk_ref, wv_ref, wg_ref, q_ref, k_ref, v_ref, g_ref = refs[len(position) :]
    sequences, residues, _ = q_ref.shape
    rows = sequences * residues
    for msg, place in zip(msgs, position):
        _, where = block_rows(place, residues)
        normed = msg[0:rows, :]
        k_ref[:, where, :] = dot(normed, wk_ref[...]).astype(BF16).reshape(q_ref.shape)
        v_ref[:, where, :] = dot(normed, wv_ref[...]).astype(BF16).reshape(q_ref.shape)
    own = msgs[0][0:rows, :]
    q_ref[...] = dot(own, wq_ref[...]).astype(BF16).reshape(q_ref.shape)
    g_ref[...] = jax.nn.sigmoid(dot(own, wg_ref[...])).reshape(g_ref.shape)


def score_kernel(heads, position, late, *refs):
    msgs = refs[: len(position)]
    q_ref, _, _, wk_ref, wv_ref, k_ref, v_ref, scored, pen_ref = refs[len(position) :]
    sequences, residues, features = q_ref.shape
    rows = sequences * residues
    total = pen_ref.shape[1]
    lane_block = iota((sequences, total), 1) // residues
    present = jnp.zeros((sequences, total), F32)
    for n, (msg, place) in enumerate(zip(msgs, position)):
        block, where = block_rows(place, residues)
        if n in late:
            normed = msg[0:rows, :]
            k_ref[:, where, :] = dot(normed, wk_ref[...]).astype(BF16).reshape(q_ref.shape)
            v_ref[:, where, :] = dot(normed, wv_ref[...]).astype(BF16).reshape(q_ref.shape)
        tiled = msg[rows : rows + sequences, :].astype(F32)
        while tiled.shape[1] < total:
            tiled = jnp.concatenate([tiled, tiled], axis=1)
        present = jnp.where(lane_block == block, tiled[:, 0:total], present)
    pen_ref[...] = (present - 1.0) * 1000000000.0
    size = features // heads
    per = LANES // size
    span = per * residues
    scale = size ** (-0.5)
    own_lanes = iota((span, LANES), 0) // residues == iota((span, LANES), 1) // size
    for s in range(sequences):
        for part in range(heads // per):
            lanes = slice(part * LANES, (part + 1) * LANES)
            stacked = jnp.concatenate([q_ref[s, :, lanes]] * per, axis=0)
            stacked = jnp.where(own_lanes, stacked, jnp.zeros_like(stacked))
            scored[s, part * span : (part + 1) * span, :] = (
                dot(stacked, k_ref[s, :, lanes], (1, 1)) * scale
            )


def attend_kernel(heads, groups, *refs):
    attend_body(heads, refs[:groups], *refs[groups:])


def attend_body(
    heads,
    biases,
    scored,
    v_ref,
    g_ref,
    pen_ref,
    arriving_ref,
    mask_ref,
    wr_ref,
    wf_ref,
    ws_ref,
    profile_ref,
    left_ref,
    right_ref,
    bias_ref,
    spread,
    bias,
    weighed,
    gated,
    leftish,
    rightish,
):
    sequences, residues, features = g_ref.shape
    total = v_ref.shape[1]
    size = features // heads
    per = LANES // size
    fit = LANES // residues
    pitch = spread.shape[1] // residues
    z_own = lax.axis_index("gx")
    for other, ref in enumerate(biases):
        bias_ref[z_own ^ other] = ref[...]
    lane = iota((heads, LANES), 1) // residues
    for i in range(residues):
        tile, inner = divmod(i, fit)
        for column in range(total // LANES):
            value = None
            for slot in range(fit):
                source = bias_ref[
                    column * fit + slot, :, tile * LANES : (tile + 1) * LANES
                ]
                shift = ((slot - inner) % fit) * residues
                if shift:
                    source = pltpu.roll(source, shift, 1)
                value = source if value is None else jnp.where(lane == slot, source, value)
            spread[column, i * pitch : i * pitch + heads, :] = value
    for column in range(total // LANES):
        for h in range(heads):
            bias[
                h * residues : (h + 1) * residues, column * LANES : (column + 1) * LANES
            ] = spread[column, pl.ds(h, residues, stride=pitch), :]
    span = per * residues
    small_lanes = [iota((residues, LANES), 1) // size == p for p in range(per)]
    parts = [
        (slice(part * LANES, (part + 1) * LANES), slice(part * span, (part + 1) * span))
        for part in range(heads // per)
    ]
    ones = jnp.ones((total, LANES), BF16)

    def weigh(s):
        penalty = pen_ref[s : s + 1, :]
        for lanes, span_rows in parts:
            scores = scored[s, span_rows, :] + bias[span_rows, :] + penalty
            top = jnp.max(scores, axis=1, keepdims=True)
            weighed[s, span_rows, :] = jnp.exp(scores - top).astype(BF16)

    def gather(s):
        for lanes, span_rows in parts:
            mixed = dot(
                weighed[s, span_rows, :], jnp.concatenate([v_ref[s, :, lanes], ones], axis=1)
            )
            value = mixed[0:residues, :]
            for p in range(1, per):
                rows = slice(p * residues, (p + 1) * residues)
                mask = jnp.concatenate([small_lanes[p], small_lanes[p]], axis=1)
                value = jnp.where(mask, mixed[rows, :], value)
            gated[s, :, lanes] = (
                g_ref[s, :, lanes] * (value[:, :LANES] / value[:, LANES:])
            ).astype(BF16)

    for step in range(sequences + LAG):
        if step < sequences:
            weigh(step)
        if step >= LAG:
            gather(step - LAG)

    rows = sequences * residues
    refreshed = (
        arriving_ref[...] + dot(gated[...].reshape(rows, features), wr_ref[...])
    ).astype(BF16)
    profile_ref[...] = refreshed.reshape(profile_ref.shape)
    normed = standardize(refreshed.astype(F32)).astype(BF16)
    width = ws_ref.shape[0]
    left_pitch, right_pitch = leftish.shape[0] // sequences, rightish.shape[0] // sequences
    sides = dot(normed, jnp.concatenate([wf_ref[...]] * (LANES // width)), (1, 1))
    for s in range(sequences):
        piece = normed[s * residues : (s + 1) * residues, :]
        leftish[s * left_pitch : s * left_pitch + residues, :] = sides[
            s * residues : (s + 1) * residues, :
        ]
        rightish[s * right_pitch : s * right_pitch + width, :] = dot(
            ws_ref[...], jnp.concatenate([piece] * fit, axis=0), (1, 1)
        )
    mask = mask_ref[...].astype(F32).astype(BF16)
    wide = residues * width
    expand = (iota((residues, wide), 1) // width == iota((residues, wide), 0)).astype(BF16)
    left_mask = dot(mask, expand)
    right_mask = dot(mask, tiling_matrix(residues, LANES))
    turns = LANES // width
    high = width // turns
    left_order = list(range(residues))
    right_order = [h * turns + low for low in range(turns) for h in range(high)]
    for tile in range(wide // LANES):
        lanes = slice(tile * LANES, (tile + 1) * LANES)
        for source, pitch, step, order, target, present in (
            (leftish, left_pitch, width, left_order, left_ref, left_mask[:, lanes]),
            (rightish, right_pitch, residues, right_order, right_ref, right_mask),
        ):
            group = iota((sequences, LANES), 1) // step
            count = LANES // step
            value = None
            for p in range(count):
                other = source[pl.ds(order[tile * count + p], sequences, stride=pitch), :]
                value = other if p == 0 else jnp.where(group == p, other, value)
            target[:, lanes] = (value * present).astype(BF16)
    left_ref[:, wide:] = right_mask.astype(BF16)
    right_ref[:, wide:] = right_mask.astype(BF16)


def pair_kernel(left_from, right_from, *refs):
    lefts = refs[: len(left_from)]
    rights = refs[len(left_from) : len(left_from) + len(right_from)]
    (pair_ref, block_ref, w1_ref, w2_ref, out_ref, left, right, flipped, rolled, spread, stacked, middle, normed) = refs[
        len(left_from) + len(right_from) :
    ]
    sequences = lefts[0].shape[0]
    rows, columns, _ = pair_ref.shape
    z_own, x_own, c_own = (lax.axis_index(n) for n in ("gx", "gy", "gz"))
    for ref, other in zip(lefts, left_from):
        start = (z_own ^ other) * sequences
        left[pl.ds(pl.multiple_of(start, sequences), sequences), :] = ref[...]
    for ref, (shift_y, shift_z, size_y, size_z) in zip(rights, right_from):
        block = lax.rem(x_own - shift_y + size_y, size_y) * size_z + lax.rem(
            c_own - shift_z + size_z, size_z
        )
        right[pl.ds(pl.multiple_of(block * sequences, sequences), sequences), :] = ref[...]
    wide = left.shape[1] - LANES
    width = wide // rows
    fit = LANES // width
    high = wide // columns // fit
    count = dot(right[:, wide:], left[:, wide:], (0, 0))[0:columns, :]
    share = 1.0 / (count + 1.0)
    tiles = wide // LANES
    deep = left.shape[0]
    span = high * columns
    flipped[...] = jnp.concatenate(
        [right[:, low * span : (low + 1) * span] for low in range(fit)]
    ).T
    group = iota((deep, LANES), 1) // width
    lane_groups = [group == q for q in range(fit)]
    for tile in range(tiles):
        lanes = slice(tile * LANES, (tile + 1) * LANES)
        chunk = left[:, lanes].astype(F32)
        for low in range(1, fit):
            rolled[low - 1, :, lanes] = pltpu.roll(chunk, low * width, 1).astype(BF16)

    def build(turn):
        for low in range(fit):
            for tile in range(tiles):
                lanes = slice(tile * LANES, (tile + 1) * LANES)
                chunk = rolled[low - 1, :, lanes] if low else left[:, lanes]
                spread[turn, low * deep : (low + 1) * deep, lanes] = jnp.where(
                    lane_groups[(low + turn) % fit], chunk, jnp.zeros_like(chunk)
                )

    def outer(turn):
        value = dot(flipped[...], spread[turn]).astype(BF16)
        for tile in range(tiles):
            for h in range(high):
                stacked[
                    turn, tile * columns : (tile + 1) * columns, h * LANES : (h + 1) * LANES
                ] = value[h * columns : (h + 1) * columns, tile * LANES : (tile + 1) * LANES]

    def mix(turn):
        mixed = dot(stacked[turn], block_ref[turn])
        for tile in range(tiles):
            i = tile * fit + turn
            where = slice(tile * columns, (tile + 1) * columns)
            middle[turn, where, :] = pair_ref[i].astype(F32) + mixed[where, :] * share[:, i : i + 1]

    def norm(turn):
        normed[turn] = standardize(middle[turn]).astype(BF16)

    def transition(turn):
        hidden = jnp.maximum(dot(normed[turn], w1_ref[...]), 0.0).astype(BF16)
        done = (middle[turn] + dot(hidden, w2_ref[...])).astype(BF16)
        for tile in range(tiles):
            out_ref[tile * fit + turn] = done[tile * columns : (tile + 1) * columns, :]

    stages = (build, outer, mix, norm, transition)
    for step in range(fit + len(stages) - 1):
        for late, stage in reversed(list(enumerate(stages))):
            if 0 <= step - late < fit:
                stage(step - late)


def local(
    sizes,
    alignment_token_ids,
    homolog_profile,
    alignment_mask,
    pair_features,
    symbol_lookup_weights,
    asking_weights,
    lookup_weights,
    content_weights,
    sigmoid_switch_weights,
    resulting_weights,
    pair_bias_matrix,
    first_factor_weights,
    second_factor_weights,
    outer_mixing_weight,
    widening_weight,
    narrowing_weight,
):
    size_x, size_y, size_z = sizes
    sequences, residues, features = homolog_profile.shape
    heads = pair_bias_matrix.shape[1]
    width = first_factor_weights.shape[1]
    pair_rows, pair_columns, pair_width = pair_features.shape
    total = residues * size_y * size_z
    rows = sequences * residues
    shape = jax.ShapeDtypeStruct

    local_pair = shape(pair_features.shape, BF16)
    local_mask = shape(alignment_mask.shape, jnp.int32)
    matrix_far = pair_bias_matrix.T
    msg, arriving, mask, pair, matrix = call(
        embed_kernel,
        (
            shape((rows + sequences, features), BF16),
            shape((rows, features), F32),
            local_mask,
            local_pair,
            shape(matrix_far.shape, F32),
        ),
        [
            pltpu.VMEM(alignment_token_ids.shape, jnp.int32),
            pltpu.VMEM(homolog_profile.shape, BF16),
            pltpu.VMEM(symbol_lookup_weights.shape, BF16),
            pltpu.VMEM((LANES, features), BF16),
            pltpu.SemaphoreType.DMA((6,)),
        ],
        flops=2 * rows * LANES * features,
        data=rows * features * 8,
        far=6,
    )(
        alignment_token_ids,
        alignment_mask,
        homolog_profile,
        symbol_lookup_weights,
        pair_features,
        matrix_far,
    )

    def shift(value, axis, count, step):
        return lax.ppermute(value, axis, [(n, (n + step) % count) for n in range(count)])

    far = [msg] + [shift(msg, "gy", size_y, r) for r in range(1, size_y)]
    position, msgs = [], []
    for r in range(size_y):
        for t in range(size_z):
            position.append((r, t, size_y, size_z))
            msgs.append(far[r] if t == 0 else shift(far[r], "gz", size_z, t))

    fit = LANES // width
    weights = (
        asking_weights,
        lookup_weights,
        content_weights,
        sigmoid_switch_weights,
        resulting_weights,
        first_factor_weights.T,
        second_factor_weights.T,
    )
    wq, wk, wv, wg, wr, wf, ws, bias_local = call(
        functools.partial(prepare_kernel, len(weights)),
        tuple(shape(w.shape, w.dtype) for w in weights)
        + (shape((heads, pair_rows * pair_columns), F32),),
        [pltpu.SemaphoreType.DMA((len(weights),))],
        flops=2 * 6 * pair_rows * pair_columns * pair_width * LANES,
        data=pair_rows * pair_columns * pair_width * 2,
        far=len(weights),
    )(*weights, pair, matrix)
    biases = [bias_local]
    for m in range(1, size_x):
        biases.append(lax.ppermute(bias_local, "gx", [(n, n ^ m) for n in range(size_x)]))

    three = (sequences, residues, features)
    keys = (sequences, total, features)
    scores = (sequences, heads * residues, total)
    late = tuple(n for n, (r, t, _, _) in enumerate(position) if r and t)
    early = tuple(n for n in range(len(position)) if n not in late)
    queries, keys_early, values_early, gates = call(
        functools.partial(project_kernel, tuple(position[n] for n in early)),
        (shape(three, BF16), shape(keys, BF16), shape(keys, BF16), shape(three, F32)),
        flops=2 * rows * features * features * 2 * (len(early) + 1),
        data=sequences * total * features * 6,
    )(*(msgs[n] for n in early), wq, wk, wv, wg)
    _, values, scored, penalty = call(
        functools.partial(score_kernel, heads, tuple(position), late),
        (
            shape(keys, BF16),
            shape(keys, BF16),
            shape(scores, F32),
            shape((sequences, total), F32),
        ),
        flops=2 * rows * features * features * 2 * len(late),
        data=sequences * total * features * 6,
        aliases={len(msgs) + 1: 0, len(msgs) + 2: 1},
    )(*msgs, queries, keys_early, values_early, wk, wv)

    wide = residues * width
    message = shape((sequences, wide + LANES), BF16)
    refreshed, left_own, right_own = call(
        functools.partial(attend_kernel, heads, size_x),
        (shape(three, BF16), message, message),
        [
            pltpu.VMEM((size_x, heads, pair_rows * pair_columns), F32),
            pltpu.VMEM((total // LANES, residues * (heads + SKEW_SMALL), LANES), F32),
            pltpu.VMEM(scores[1:], F32),
            pltpu.VMEM(scores, BF16),
            pltpu.VMEM(three, BF16),
            pltpu.VMEM((sequences * (residues + SKEW), LANES), F32),
            pltpu.VMEM((sequences * (width + SKEW), LANES), F32),
        ],
        flops=4 * sequences * heads * residues * total * LANES,
        data=sequences * total * features * 4,
    )(*biases, scored, values, gates, penalty, arriving, mask, wr, wf, ws)

    lefts = [left_own]
    for m in range(1, size_x):
        lefts.append(lax.ppermute(left_own, "gx", [(n, n ^ m) for n in range(size_x)]))
    right_from, rights = [], []
    blocks = size_y * size_z
    for r in range(size_y):
        pairs = []
        for a in range(size_x):
            for b in range(blocks):
                to = ((a // size_z + r) % size_y) * size_z + a % size_z
                pairs.append((a * blocks + b, b * blocks + to))
        got = lax.ppermute(right_own, ("gx", "gy", "gz"), pairs)
        for t in range(size_z):
            right_from.append((r, t, size_y, size_z))
            rights.append(got if t == 0 else shift(got, "gz", size_z, t))

    mixing = (outer_mixing_weight, widening_weight, narrowing_weight)
    block, w1, w2, refreshed = call(
        block_kernel,
        (shape((fit, width * width, pair_width), BF16),)
        + tuple(shape(w.shape, w.dtype) for w in mixing[1:])
        + (shape(three, BF16),),
        [
            pltpu.VMEM(outer_mixing_weight.shape, BF16),
            pltpu.VMEM((width * (width + SKEW), pair_width), F32),
            pltpu.SemaphoreType.DMA((len(mixing) + 1,)),
        ],
        data=width * width * fit * pair_width * 2,
        far=len(mixing),
        sent=(3,),
    )(*mixing, refreshed)

    depth = sequences * size_x
    (pair_output,) = call(
        functools.partial(pair_kernel, tuple(range(size_x)), tuple(right_from)),
        (shape(pair_features.shape, BF16),),
        [
            pltpu.VMEM((depth, wide + LANES), BF16),
            pltpu.VMEM((depth, wide + LANES), BF16),
            pltpu.VMEM((width // fit * pair_columns, fit * depth), BF16),
            pltpu.VMEM((fit - 1, depth, wide), BF16),
            pltpu.VMEM((fit, fit * depth, wide), BF16),
            pltpu.VMEM((fit, pair_rows // fit * pair_columns, width * width), BF16),
            pltpu.VMEM((fit, pair_rows // fit * pair_columns, pair_width), F32),
            pltpu.VMEM((fit, pair_rows // fit * pair_columns, pair_width), BF16),
        ],
        flops=2 * pair_rows * pair_columns * width * width * pair_width * fit,
        data=width * width * fit * pair_width * fit * 2,
    )(*lefts, *rights, pair, block, w1, w2)
    return refreshed, pair_output


def solution(mesh):
    sizes = tuple(mesh.shape[name] for name in ("gx", "gy", "gz"))
    assert sizes[0] == sizes[1] * sizes[2] and sizes[0] & (sizes[0] - 1) == 0
    in_specs = (
        P(("grp", "gx"), ("gy", "gz")),
        P(("grp", "gx"), ("gy", "gz"), None),
        P(("grp", "gx"), ("gy", "gz")),
        P(("grp", "gy", "gz"), "gx", None),
    ) + (P(),) * 12
    out_specs = (P(("grp", "gx"), ("gy", "gz"), None), P(("grp", "gy", "gz"), "gx", None))

    def body(*args):
        return local(sizes, *args)

    return jax.shard_map(
        body, mesh=mesh, in_specs=in_specs, out_specs=out_specs, check_vma=False
    )
```

```python
import functools
import math

import jax
import jax.numpy as jnp
from jax import lax
from jax.experimental import pallas as pl
from jax.experimental.pallas import tpu as pltpu
from jax.sharding import PartitionSpec as P


LANES = 128
LAG = 8
SKEW = 4
SKEW_SMALL = 1
F32 = jnp.float32
BF16 = jnp.bfloat16


def iota(shape, dim):
    return lax.broadcasted_iota(jnp.int32, shape, dim)


def standardize(values):
    average = jnp.mean(values, axis=-1, keepdims=True)
    centred = values - average
    return centred * lax.rsqrt(jnp.mean(centred * centred, axis=-1, keepdims=True) + 1e-05)


def dot(left, right, contract=(1, 0), precision=None):
    return lax.dot_general(
        left,
        right,
        (((contract[0],), (contract[1],)), ((), ())),
        preferred_element_type=F32,
        precision=precision,
    )


def tiling_matrix(rows, columns):
    return (iota((rows, columns), 1) % rows == iota((rows, columns), 0)).astype(BF16)


def call(body, outs, scratch=(), flops=0, data=0, far=0, aliases={}, sent=()):
    near = pl.BlockSpec(memory_space=pltpu.VMEM)
    held = sum(
        math.prod(ref.shape) * jnp.dtype(ref.dtype).itemsize
        for ref in scratch
        if hasattr(ref, "shape") and ref.memory_space == pltpu.VMEM
    )

    def run(*operands):
        operands = [
            pltpu.with_memory_space_constraint(x, pltpu.HBM) if n < far else x
            for n, x in enumerate(operands)
        ]
        return pl.pallas_call(
            body,
            out_shape=outs,
            in_specs=[pl.BlockSpec(memory_space=pltpu.HBM)] * far + [near] * (len(operands) - far),
            out_specs=[
                pl.BlockSpec(memory_space=pltpu.HBM) if n in sent else near
                for n in range(len(outs))
            ],
            scratch_shapes=scratch,
            cost_estimate=pl.CostEstimate(flops=flops, bytes_accessed=data, transcendentals=0),
            compiler_params=pltpu.CompilerParams(vmem_limit_bytes=held * 5 // 4 + (6 << 20)),
            input_output_aliases=aliases,
        )(*operands)

    return run


def fetch(sources, targets, sems):
    copies = [
        pltpu.make_async_copy(source, target, sems.at[n])
        for n, (source, target) in enumerate(zip(sources, targets))
    ]
    for copy in copies:
        copy.start()
    return copies


def embed_kernel(
    ids_far,
    mask_far,
    profile_far,
    table_far,
    pair_far,
    matrix_far,
    msg_ref,
    arriving_ref,
    mask_ref,
    pair_ref,
    matrix_ref,
    ids_ref,
    profile_ref,
    table_ref,
    padded,
    sems,
):
    copies = fetch(
        (ids_far, table_far, mask_far, profile_far, pair_far, matrix_far),
        (ids_ref, table_ref, mask_ref, profile_ref, pair_ref, matrix_ref),
        sems,
    )
    sequences, residues, features = profile_ref.shape
    kinds = table_ref.shape[0]
    for copy in copies[:3]:
        copy.wait()
    padded[...] = jnp.zeros_like(padded)
    padded[0:kinds, :] = table_ref[...]
    columns = ids_ref[...].astype(F32).T
    labels = iota((residues, padded.shape[0]), 1).astype(F32)
    rows = sequences * residues
    mask = mask_ref[...].astype(F32).astype(BF16)
    msg_ref[rows:, :] = dot(mask, tiling_matrix(residues, features)).astype(BF16)
    table = padded[...]
    copies[3].wait()
    step = 4
    for start in range(0, sequences, step):
        hot = [
            (columns[:, s : s + 1] == labels).astype(F32).astype(BF16)
            for s in range(start, start + step)
        ]
        where = slice(start * residues, (start + step) * residues)
        profile = profile_ref[start : start + step].reshape(step * residues, features)
        arriving = profile.astype(F32) + dot(jnp.concatenate(hot, axis=0), table)
        arriving_ref[where, :] = arriving
        msg_ref[where, :] = standardize(arriving).astype(BF16)
    for copy in copies[4:]:
        copy.wait()


def thirds(values):
    high = values.astype(BF16)
    rest = values - high.astype(F32)
    middle = rest.astype(BF16)
    return [high, middle, (rest - middle.astype(F32)).astype(BF16)]


def prepare_kernel(weights, *refs):
    far, refs = refs[:weights], refs[weights:]
    (pair_ref, matrix_ref, mask_ref), refs = refs[:3], refs[3:]
    near, (out_ref, sems) = refs[:weights], refs[weights:]
    copies = fetch(far, near, sems)
    rows, columns, width = pair_ref.shape
    matrix = thirds(matrix_ref[...])
    stacked = jnp.concatenate([jnp.concatenate(matrix, axis=0)] * len(matrix), axis=1)
    heads = matrix_ref.shape[0]
    sequences, residues = mask_ref.shape
    out_ref[:, rows * columns :] = jnp.zeros((heads, LANES), F32)
    for n in range(sequences // heads):
        lane = rows * columns + n * residues
        out_ref[:, lane : lane + residues] = mask_ref[n * heads : (n + 1) * heads, :].astype(F32)
    step = LANES // columns
    for start in range(0, rows, step):
        part = pair_ref[start : start + step].reshape(step * columns, width).astype(F32)
        products = dot(stacked, jnp.concatenate(thirds(standardize(part)), axis=1), (1, 1))
        bias = products[2 * heads :] + products[heads : 2 * heads] + products[:heads]
        out_ref[:, start * columns : (start + step) * columns] = bias
    for copy in copies:
        copy.wait()


def block_kernel(
    mix_far, w1_far, w2_far, profile_ref, block_ref, w1_ref, w2_ref, profile_far, mix_ref, wide, sems
):
    copies = fetch(
        (mix_far, w1_far, w2_far, profile_ref), (mix_ref, w1_ref, w2_ref, profile_far), sems
    )
    copies[0].wait()
    turns = block_ref.shape[0]
    width = other = math.isqrt(mix_ref.shape[0])
    pitch = wide.shape[0] // width
    for c in range(width):
        wide[c * pitch : c * pitch + other, :] = mix_ref[c * other : (c + 1) * other, :].astype(F32)
    for d in range(other):
        piece = wide[pl.ds(d, width, stride=pitch), :].astype(BF16)
        high, low = divmod(d, turns)
        for turn in range(turns):
            spot = (high * turns + (low + turn) % turns) * width
            block_ref[turn, spot : spot + width, :] = piece
    for copy in copies[1:]:
        copy.wait()


def block_rows(shift, residues):
    shift_y, shift_z, size_y, size_z = shift
    block = lax.rem(lax.axis_index("gy") - shift_y + size_y, size_y) * size_z + lax.rem(
        lax.axis_index("gz") - shift_z + size_z, size_z
    )
    return block, pl.ds(pl.multiple_of(block * residues, residues), residues)


def project_kernel(position, *refs):
    msgs = refs[: len(position)]
    wq_ref, wk_ref, wv_ref, wg_ref, q_ref, k_ref, v_ref, g_ref = refs[len(position) :]
    sequences, residues, _ = q_ref.shape
    rows = sequences * residues
    for msg, place in zip(msgs, position):
        _, where = block_rows(place, residues)
        normed = msg[0:rows, :]
        k_ref[:, where, :] = dot(normed, wk_ref[...]).astype(BF16).reshape(q_ref.shape)
        v_ref[:, where, :] = dot(normed, wv_ref[...]).astype(BF16).reshape(q_ref.shape)
    own = msgs[0][0:rows, :]
    q_ref[...] = dot(own, wq_ref[...]).astype(BF16).reshape(q_ref.shape)
    g_ref[...] = jax.nn.sigmoid(dot(own, wg_ref[...])).reshape(g_ref.shape)


def score_kernel(heads, position, late, *refs):
    msgs = refs[: len(position)]
    q_ref, _, _, wk_ref, wv_ref, k_ref, v_ref, scored, pen_ref = refs[len(position) :]
    sequences, residues, features = q_ref.shape
    rows = sequences * residues
    total = pen_ref.shape[1]
    lane_block = iota((sequences, total), 1) // residues
    present = jnp.zeros((sequences, total), F32)
    for n, (msg, place) in enumerate(zip(msgs, position)):
        block, where = block_rows(place, residues)
        if n in late:
            normed = msg[0:rows, :]
            k_ref[:, where, :] = dot(normed, wk_ref[...]).astype(BF16).reshape(q_ref.shape)
            v_ref[:, where, :] = dot(normed, wv_ref[...]).astype(BF16).reshape(q_ref.shape)
        tiled = msg[rows : rows + sequences, :].astype(F32)
        while tiled.shape[1] < total:
            tiled = jnp.concatenate([tiled, tiled], axis=1)
        present = jnp.where(lane_block == block, tiled[:, 0:total], present)
    pen_ref[...] = (present - 1.0) * 1000000000.0
    size = features // heads
    per = LANES // size
    span = per * residues
    scale = size ** (-0.5)
    own_lanes = iota((span, LANES), 0) // residues == iota((span, LANES), 1) // size
    for s in range(sequences):
        for part in range(heads // per):
            lanes = slice(part * LANES, (part + 1) * LANES)
            stacked = jnp.concatenate([q_ref[s, :, lanes]] * per, axis=0)
            stacked = jnp.where(own_lanes, stacked, jnp.zeros_like(stacked))
            scored[s, part * span : (part + 1) * span, :] = (
                dot(stacked, k_ref[s, :, lanes], (1, 1)) * scale
            )


def attend_kernel(heads, groups, *refs):
    attend_body(heads, refs[:groups], *refs[groups:])


def attend_body(
    heads,
    biases,
    scored,
    v_ref,
    g_ref,
    pen_ref,
    arriving_ref,
    mask_ref,
    wr_ref,
    wf_ref,
    ws_ref,
    profile_ref,
    left_ref,
    right_ref,
    bias_ref,
    spread,
    bias,
    weighed,
    gated,
    leftish,
    rightish,
):
    sequences, residues, features = g_ref.shape
    total = v_ref.shape[1]
    size = features // heads
    per = LANES // size
    fit = LANES // residues
    pitch = spread.shape[1] // residues
    z_own = lax.axis_index("gx")
    for other, ref in enumerate(biases):
        bias_ref[z_own ^ other] = ref[:, : bias_ref.shape[2]]
    lane = iota((heads, LANES), 1) // residues
    for i in range(residues):
        tile, inner = divmod(i, fit)
        for column in range(total // LANES):
            value = None
            for slot in range(fit):
                source = bias_ref[
                    column * fit + slot, :, tile * LANES : (tile + 1) * LANES
                ]
                shift = ((slot - inner) % fit) * residues
                if shift:
                    source = pltpu.roll(source, shift, 1)
                value = source if value is None else jnp.where(lane == slot, source, value)
            spread[column, i * pitch : i * pitch + heads, :] = value
    for column in range(total // LANES):
        for h in range(heads):
            bias[
                h * residues : (h + 1) * residues, column * LANES : (column + 1) * LANES
            ] = spread[column, pl.ds(h, residues, stride=pitch), :]
    span = per * residues
    small_lanes = [iota((residues, LANES), 1) // size == p for p in range(per)]
    parts = [
        (slice(part * LANES, (part + 1) * LANES), slice(part * span, (part + 1) * span))
        for part in range(heads // per)
    ]
    ones = jnp.ones((total, LANES), BF16)

    def weigh(s):
        penalty = pen_ref[s : s + 1, :]
        for lanes, span_rows in parts:
            scores = scored[s, span_rows, :] + bias[span_rows, :] + penalty
            top = jnp.max(scores, axis=1, keepdims=True)
            weighed[s, span_rows, :] = jnp.exp(scores - top).astype(BF16)

    def gather(s):
        for lanes, span_rows in parts:
            mixed = dot(
                weighed[s, span_rows, :], jnp.concatenate([v_ref[s, :, lanes], ones], axis=1)
            )
            value = mixed[0:residues, :]
            for p in range(1, per):
                rows = slice(p * residues, (p + 1) * residues)
                mask = jnp.concatenate([small_lanes[p], small_lanes[p]], axis=1)
                value = jnp.where(mask, mixed[rows, :], value)
            gated[s, :, lanes] = (
                g_ref[s, :, lanes] * (value[:, :LANES] / value[:, LANES:])
            ).astype(BF16)

    for step in range(sequences + LAG):
        if step < sequences:
            weigh(step)
        if step >= LAG:
            gather(step - LAG)

    rows = sequences * residues
    refreshed = (
        arriving_ref[...] + dot(gated[...].reshape(rows, features), wr_ref[...])
    ).astype(BF16)
    profile_ref[...] = refreshed.reshape(profile_ref.shape)
    normed = standardize(refreshed.astype(F32)).astype(BF16)
    width = ws_ref.shape[0]
    left_pitch, right_pitch = leftish.shape[0] // sequences, rightish.shape[0] // sequences
    sides = dot(normed, jnp.concatenate([wf_ref[...]] * (LANES // width)), (1, 1))
    for s in range(sequences):
        piece = normed[s * residues : (s + 1) * residues, :]
        leftish[s * left_pitch : s * left_pitch + residues, :] = sides[
            s * residues : (s + 1) * residues, :
        ]
        rightish[s * right_pitch : s * right_pitch + width, :] = dot(
            ws_ref[...], jnp.concatenate([piece] * fit, axis=0), (1, 1)
        )
    mask = mask_ref[...].astype(F32).astype(BF16)
    wide = residues * width
    expand = (iota((residues, wide), 1) // width == iota((residues, wide), 0)).astype(BF16)
    left_mask = dot(mask, expand)
    right_mask = dot(mask, tiling_matrix(residues, LANES))
    turns = LANES // width
    high = width // turns
    left_order = list(range(residues))
    right_order = [h * turns + low for low in range(turns) for h in range(high)]
    for tile in range(wide // LANES):
        lanes = slice(tile * LANES, (tile + 1) * LANES)
        for source, pitch, step, order, target, present in (
            (leftish, left_pitch, width, left_order, left_ref, left_mask[:, lanes]),
            (rightish, right_pitch, residues, right_order, right_ref, right_mask),
        ):
            group = iota((sequences, LANES), 1) // step
            count = LANES // step
            value = None
            for p in range(count):
                other = source[pl.ds(order[tile * count + p], sequences, stride=pitch), :]
                value = other if p == 0 else jnp.where(group == p, other, value)
            target[:, lanes] = (value * present).astype(BF16)
    right_ref[:, wide:] = right_mask.astype(BF16)


def pair_kernel(left_from, right_from, *refs):
    biases, refs = refs[: len(left_from)], refs[len(left_from) :]
    lefts = refs[: len(left_from)]
    rights = refs[len(left_from) : len(left_from) + len(right_from)]
    (pair_ref, block_ref, w1_ref, w2_ref, out_ref, left, right, flipped, rolled, spread, stacked, middle, normed, present) = refs[
        len(left_from) + len(right_from) :
    ]
    sequences = lefts[0].shape[0]
    rows, columns, _ = pair_ref.shape
    z_own, x_own, c_own = (lax.axis_index(n) for n in ("gx", "gy", "gz"))
    for ref, other in zip(lefts, left_from):
        start = (z_own ^ other) * sequences
        left[pl.ds(pl.multiple_of(start, sequences), sequences), :] = ref[...]
    for ref, (shift_y, shift_z, size_y, size_z) in zip(rights, right_from):
        block = lax.rem(x_own - shift_y + size_y, size_y) * size_z + lax.rem(
            c_own - shift_z + size_z, size_z
        )
        right[pl.ds(pl.multiple_of(block * sequences, sequences), sequences), :] = ref[...]
    wide = left.shape[1]
    heads = biases[0].shape[0]
    for other, ref in enumerate(biases):
        for n in range(sequences // heads):
            start = (z_own ^ other) * sequences + n * heads
            mask = ref[:, ref.shape[1] - LANES :]
            present[pl.ds(pl.multiple_of(start, heads), heads), :] = (
                pltpu.roll(mask, LANES - n * rows, 1) if n else mask
            )
    width = wide // rows
    fit = LANES // width
    high = wide // columns // fit
    count = dot(right[:, wide:], present[...].astype(BF16), (0, 0))[0:columns, :]
    share = 1.0 / (count + 1.0)
    tiles = wide // LANES
    deep = left.shape[0]
    span = high * columns
    flipped[...] = jnp.concatenate(
        [right[:, low * span : (low + 1) * span] for low in range(fit)]
    ).T
    group = iota((deep, LANES), 1) // width
    lane_groups = [group == q for q in range(fit)]
    for tile in range(tiles):
        lanes = slice(tile * LANES, (tile + 1) * LANES)
        chunk = left[:, lanes].astype(F32)
        for low in range(1, fit):
            rolled[low - 1, :, lanes] = pltpu.roll(chunk, low * width, 1).astype(BF16)

    def build(turn):
        for low in range(fit):
            for tile in range(tiles):
                lanes = slice(tile * LANES, (tile + 1) * LANES)
                chunk = rolled[low - 1, :, lanes] if low else left[:, lanes]
                spread[turn, low * deep : (low + 1) * deep, lanes] = jnp.where(
                    lane_groups[(low + turn) % fit], chunk, jnp.zeros_like(chunk)
                )

    def outer(turn):
        value = dot(flipped[...], spread[turn]).astype(BF16)
        for tile in range(tiles):
            for h in range(high):
                stacked[
                    turn, tile * columns : (tile + 1) * columns, h * LANES : (h + 1) * LANES
                ] = value[h * columns : (h + 1) * columns, tile * LANES : (tile + 1) * LANES]

    def mix(turn):
        mixed = dot(stacked[turn], block_ref[turn])
        for tile in range(tiles):
            i = tile * fit + turn
            where = slice(tile * columns, (tile + 1) * columns)
            middle[turn, where, :] = pair_ref[i].astype(F32) + mixed[where, :] * share[:, i : i + 1]

    def norm(turn):
        normed[turn] = standardize(middle[turn]).astype(BF16)

    def transition(turn):
        hidden = jnp.maximum(dot(normed[turn], w1_ref[...]), 0.0).astype(BF16)
        done = (middle[turn] + dot(hidden, w2_ref[...])).astype(BF16)
        for tile in range(tiles):
            out_ref[tile * fit + turn] = done[tile * columns : (tile + 1) * columns, :]

    stages = (build, outer, mix, norm, transition)
    for step in range(fit + len(stages) - 1):
        for late, stage in reversed(list(enumerate(stages))):
            if 0 <= step - late < fit:
                stage(step - late)


def local(
    sizes,
    alignment_token_ids,
    homolog_profile,
    alignment_mask,
    pair_features,
    symbol_lookup_weights,
    asking_weights,
    lookup_weights,
    content_weights,
    sigmoid_switch_weights,
    resulting_weights,
    pair_bias_matrix,
    first_factor_weights,
    second_factor_weights,
    outer_mixing_weight,
    widening_weight,
    narrowing_weight,
):
    size_x, size_y, size_z = sizes
    sequences, residues, features = homolog_profile.shape
    heads = pair_bias_matrix.shape[1]
    width = first_factor_weights.shape[1]
    pair_rows, pair_columns, pair_width = pair_features.shape
    total = residues * size_y * size_z
    rows = sequences * residues
    shape = jax.ShapeDtypeStruct

    local_pair = shape(pair_features.shape, BF16)
    local_mask = shape(alignment_mask.shape, jnp.int32)
    matrix_far = pair_bias_matrix.T
    msg, arriving, mask, pair, matrix = call(
        embed_kernel,
        (
            shape((rows + sequences, features), BF16),
            shape((rows, features), F32),
            local_mask,
            local_pair,
            shape(matrix_far.shape, F32),
        ),
        [
            pltpu.VMEM(alignment_token_ids.shape, jnp.int32),
            pltpu.VMEM(homolog_profile.shape, BF16),
            pltpu.VMEM(symbol_lookup_weights.shape, BF16),
            pltpu.VMEM((LANES, features), BF16),
            pltpu.SemaphoreType.DMA((6,)),
        ],
        flops=2 * rows * LANES * features,
        data=rows * features * 8,
        far=6,
    )(
        alignment_token_ids,
        alignment_mask,
        homolog_profile,
        symbol_lookup_weights,
        pair_features,
        matrix_far,
    )

    def shift(value, axis, count, step):
        return lax.ppermute(value, axis, [(n, (n + step) % count) for n in range(count)])

    far = [msg] + [shift(msg, "gy", size_y, r) for r in range(1, size_y)]
    position, msgs = [], []
    for r in range(size_y):
        for t in range(size_z):
            position.append((r, t, size_y, size_z))
            msgs.append(far[r] if t == 0 else shift(far[r], "gz", size_z, t))

    fit = LANES // width
    weights = (
        asking_weights,
        lookup_weights,
        content_weights,
        sigmoid_switch_weights,
        resulting_weights,
        first_factor_weights.T,
        second_factor_weights.T,
    )
    wq, wk, wv, wg, wr, wf, ws, bias_local = call(
        functools.partial(prepare_kernel, len(weights)),
        tuple(shape(w.shape, w.dtype) for w in weights)
        + (shape((heads, pair_rows * pair_columns + LANES), F32),),
        [pltpu.SemaphoreType.DMA((len(weights),))],
        flops=2 * 6 * pair_rows * pair_columns * pair_width * LANES,
        data=pair_rows * pair_columns * pair_width * 2,
        far=len(weights),
    )(*weights, pair, matrix, mask)
    biases = [bias_local]
    for m in range(1, size_x):
        biases.append(lax.ppermute(bias_local, "gx", [(n, n ^ m) for n in range(size_x)]))

    three = (sequences, residues, features)
    keys = (sequences, total, features)
    scores = (sequences, heads * residues, total)
    late = tuple(n for n, (r, t, _, _) in enumerate(position) if r and t)
    early = tuple(n for n in range(len(position)) if n not in late)
    queries, keys_early, values_early, gates = call(
        functools.partial(project_kernel, tuple(position[n] for n in early)),
        (shape(three, BF16), shape(keys, BF16), shape(keys, BF16), shape(three, F32)),
        flops=2 * rows * features * features * 2 * (len(early) + 1),
        data=sequences * total * features * 6,
    )(*(msgs[n] for n in early), wq, wk, wv, wg)
    _, values, scored, penalty = call(
        functools.partial(score_kernel, heads, tuple(position), late),
        (
            shape(keys, BF16),
            shape(keys, BF16),
            shape(scores, F32),
            shape((sequences, total), F32),
        ),
        flops=2 * rows * features * features * 2 * len(late),
        data=sequences * total * features * 6,
        aliases={len(msgs) + 1: 0, len(msgs) + 2: 1},
    )(*msgs, queries, keys_early, values_early, wk, wv)

    wide = residues * width
    message = shape((sequences, wide + LANES), BF16)
    refreshed, left_own, right_own = call(
        functools.partial(attend_kernel, heads, size_x),
        (shape(three, BF16), shape((sequences, wide), BF16), message),
        [
            pltpu.VMEM((size_x, heads, pair_rows * pair_columns), F32),
            pltpu.VMEM((total // LANES, residues * (heads + SKEW_SMALL), LANES), F32),
            pltpu.VMEM(scores[1:], F32),
            pltpu.VMEM(scores, BF16),
            pltpu.VMEM(three, BF16),
            pltpu.VMEM((sequences * (residues + SKEW), LANES), F32),
            pltpu.VMEM((sequences * (width + SKEW), LANES), F32),
        ],
        flops=4 * sequences * heads * residues * total * LANES,
        data=sequences * total * features * 4,
    )(*biases, scored, values, gates, penalty, arriving, mask, wr, wf, ws)

    lefts = [left_own]
    for m in range(1, size_x):
        lefts.append(lax.ppermute(left_own, "gx", [(n, n ^ m) for n in range(size_x)]))
    right_from, rights = [], []
    blocks = size_y * size_z
    for r in range(size_y):
        pairs = []
        for a in range(size_x):
            for b in range(blocks):
                to = ((a // size_z + r) % size_y) * size_z + a % size_z
                pairs.append((a * blocks + b, b * blocks + to))
        got = lax.ppermute(right_own, ("gx", "gy", "gz"), pairs)
        for t in range(size_z):
            right_from.append((r, t, size_y, size_z))
            rights.append(got if t == 0 else shift(got, "gz", size_z, t))

    mixing = (outer_mixing_weight, widening_weight, narrowing_weight)
    block, w1, w2, refreshed = call(
        block_kernel,
        (shape((fit, width * width, pair_width), BF16),)
        + tuple(shape(w.shape, w.dtype) for w in mixing[1:])
        + (shape(three, BF16),),
        [
            pltpu.VMEM(outer_mixing_weight.shape, BF16),
            pltpu.VMEM((width * (width + SKEW), pair_width), F32),
            pltpu.SemaphoreType.DMA((len(mixing) + 1,)),
        ],
        data=width * width * fit * pair_width * 2,
        far=len(mixing),
        sent=(3,),
    )(*mixing, refreshed)

    depth = sequences * size_x
    (pair_output,) = call(
        functools.partial(pair_kernel, tuple(range(size_x)), tuple(right_from)),
        (shape(pair_features.shape, BF16),),
        [
            pltpu.VMEM((depth, wide), BF16),
            pltpu.VMEM((depth, wide + LANES), BF16),
            pltpu.VMEM((width // fit * pair_columns, fit * depth), BF16),
            pltpu.VMEM((fit - 1, depth, wide), BF16),
            pltpu.VMEM((fit, fit * depth, wide), BF16),
            pltpu.VMEM((fit, pair_rows // fit * pair_columns, width * width), BF16),
            pltpu.VMEM((fit, pair_rows // fit * pair_columns, pair_width), F32),
            pltpu.VMEM((fit, pair_rows // fit * pair_columns, pair_width), BF16),
            pltpu.VMEM((depth, LANES), F32),
        ],
        flops=2 * pair_rows * pair_columns * width * width * pair_width * fit,
        data=width * width * fit * pair_width * fit * 2,
    )(*biases, *lefts, *rights, pair, block, w1, w2)
    return refreshed, pair_output


def solution(mesh):
    sizes = tuple(mesh.shape[name] for name in ("gx", "gy", "gz"))
    assert sizes[0] == sizes[1] * sizes[2] and sizes[0] & (sizes[0] - 1) == 0
    in_specs = (
        P(("grp", "gx"), ("gy", "gz")),
        P(("grp", "gx"), ("gy", "gz"), None),
        P(("grp", "gx"), ("gy", "gz")),
        P(("grp", "gy", "gz"), "gx", None),
    ) + (P(),) * 12
    out_specs = (P(("grp", "gx"), ("gy", "gz"), None), P(("grp", "gy", "gz"), "gx", None))

    def body(*args):
        return local(sizes, *args)

    return jax.shard_map(
        body, mesh=mesh, in_specs=in_specs, out_specs=out_specs, check_vma=False
    )
```
